32 devices in a mesh: parts: 2 (over x), space: 16 (over z, y, core).
Axes of the slice: x: 2, y: 2, z: 4, core: 2. Of those that a mesh axis runs over, the one named last changes fastest.
Arguments:
- coefficients: bfloat16 [64, 4096], P('parts'), parts along dimension 0, may hold values from -6 to 6
- kl_modes: bfloat16 [8192, 2048], P('parts', 'space'), parts along dimension 0, may hold values from -0.09375 to 0.09375
- green: bfloat16 [4096, 256, 128], P(('parts', 'space')), parts along dimension 0, may hold values from -0.1875 to 0.1875
- sub_index: int32 [4096], P('parts'), parts along dimension 0, may hold values from 0 to 2047, each once
- kernel: float32 [33, 33], replicated, may hold values from 0.2 to 5
- wet_mask: int32 [512, 128], P(('parts', 'space')), parts along dimension 0, may hold values 0 or 1
Outputs:
- surface: float32 [64, 256, 128], P('parts', 'space'), parts along dimension 0
The draws below stay inside these ranges and needn't reach their ends.
There are 2 independent parts, one for each index of `parts`. The reference program is written for one: setup_inputs(seed, part) draws one part's arguments, and reference() takes and returns one part's arrays. A program takes and returns all parts, laid end to end along the dimension named above; an argument that names none is the same for every part. Nothing has to cross between parts.
Inputs may be any that keep to these rules, and one draw needn't show every extreme that they name: `sub_index`: each subfault appears once.
All inputs are finite; a program needn't handle non-finite values. No bound on the sum of `wet_mask` on one device may be relied on, other than what follows from the above.
Results may differ from the reference program's by a relative error of at most 0.005.
Values may be sent and summed in bfloat16 or wider, within the bound.
No kernel may reach another device: no remote copies, remote signals or barrier semaphores. Data moves between devices by JAX's collectives and lax.ppermute only.
A program may use at most 128 MiB of HBM per device.

```python
import math
import jax
import jax.numpy as jnp
from jax import lax

R = 32
M = 4096
S = 2048
CX = 16
NY = 128
HALF = 16
TAPS = 33
NX = 256


def set_ends(drawn, own_key, smallest, top_value):
    place = [jax.random.randint(jax.random.fold_in(own_key, axis), (), 0, length) for axis, length in enumerate(drawn.shape)]
    longest = drawn.shape.index(max(drawn.shape))
    next_to = place[:longest] + [(place[longest] + 1) % drawn.shape[longest]] + place[longest + 1:]
    return drawn.at[tuple(place)].set(smallest).at[tuple(next_to)].set(top_value)


def spiked(result, rng, source, target, blocks, factor):
    owner, partner = [(jnp.arange(result.shape[dim]) // (result.shape[dim] // blocks)).reshape([-1 if axis == dim else 1 for axis in range(result.ndim)]) for dim in (source, target)]
    chosen = jax.random.permutation(rng, blocks)[partner]
    strong = (owner == chosen) | (owner == (partner + blocks // 2) % blocks)
    return jnp.where(strong, factor * result, result)


def block_levels(stream_key, shape, split, least, largest):
    level, own = 1.0, jax.random.fold_in(stream_key, 6)
    for dim, shards_of in split:
        steps = jnp.exp(jax.random.uniform(jax.random.fold_in(own, dim), (shards_of,), jnp.float32, least / len(split), largest / len(split)))
        level = level * jnp.repeat(steps, shape[dim] // shards_of).reshape([-1 if axis == dim else 1 for axis in range(len(shape))])
    return level


def bell_draw(rng, dims, scale, most, shards=(), kind=jnp.bfloat16):
    values = scale * jax.random.normal(rng, dims, jnp.float32)
    if shards:
        values = values * block_levels(rng, dims, shards, -0.22, 0.18)
    return jnp.clip(values, -most, most).astype(kind)


def bell_draw_with(rng, extent, spread, bound, shards, heavy, kind=jnp.bfloat16):
    entries = spread * jax.random.normal(rng, extent, jnp.float32)
    if shards:
        entries = entries * block_levels(rng, extent, shards, -0.22, 0.18)
    return jnp.clip(spiked(entries, jax.random.fold_in(rng, 3), *heavy), -bound, bound).astype(kind)


def setup_inputs(seed: int = 0, part: int = 0) -> dict:
    splits = jax.random.split(jax.random.key(seed), 7)
    part_splits = jax.random.split(jax.random.fold_in(splits[6], part), 7)
    coefficients = bell_draw(part_splits[0], (R, M), 1.0, 6.0)
    kl_modes = bell_draw(part_splits[1], (M, S), M ** -0.5, 0.09375, ((1, 16),))
    green = bell_draw_with(part_splits[2], (S, NX, NY), S ** -0.5, 0.1875, ((0, 16),), (0, 1, 16, 2.0))
    sub_index = jax.random.permutation(part_splits[3], S).astype(jnp.int32)
    kernel = jnp.clip(jnp.exp(jax.random.uniform(splits[4], (TAPS, TAPS), jnp.float32, math.log(0.2), math.log(5.0))), 0.2, 5.0)
    wet_mask = set_ends((jax.random.randint(part_splits[5], (NX, NY), 0, 4) < 3).astype(jnp.int32), jax.random.fold_in(part_splits[5], 1), 0, 1)
    return dict(coefficients=coefficients, kl_modes=kl_modes, green=green, sub_index=sub_index, kernel=kernel, wet_mask=wet_mask)


def make_bands(weights, width):
    half = weights.shape[1] // 2
    source = lax.broadcasted_iota(jnp.int32, (width, width), 0)
    target = lax.broadcasted_iota(jnp.int32, (width, width), 1)
    offset = source - target + half
    inside = (offset >= 0) & (offset <= 2 * half)
    picked = jnp.take(weights, jnp.clip(offset, 0, 2 * half).astype(jnp.int32), axis=1)
    return jnp.where(inside[None], picked, jnp.zeros_like(picked))


def reference(coefficients, kl_modes, green, sub_index, kernel, wet_mask):
    field = jnp.dot(coefficients, kl_modes, preferred_element_type=jnp.float32)
    slip = jnp.exp(0.5 * field).astype(jnp.bfloat16)
    slip_rows = jnp.take(slip, sub_index, axis=1).astype(jnp.float32)

    def block(index):
        tile = lax.dynamic_slice_in_dim(green, index * CX, CX, 1).astype(jnp.float32)
        return jnp.dot(slip_rows, tile.reshape(S, CX * NY), precision=lax.Precision.HIGHEST)

    blocks = lax.map(block, jnp.arange(NX // CX, dtype=jnp.int32))
    uplift = blocks.reshape(NX // CX, R, CX, NY).transpose(1, 0, 2, 3).reshape(R, NX, NY)
    seafloor = uplift.astype(jnp.bfloat16).astype(jnp.float32)
    weights = (kernel / jnp.sum(kernel)).astype(jnp.bfloat16).astype(jnp.float32)
    bands = make_bands(weights, NY)
    padded = jnp.pad(seafloor, ((0, 0), (HALF, HALF), (0, 0)))
    smooth = jnp.zeros((R * NX, NY), jnp.float32)
    for shift_row in range(TAPS):
        rows = padded[:, shift_row:shift_row + NX, :].reshape(R * NX, NY)
        smooth = smooth + jnp.dot(rows, bands[shift_row], precision=lax.Precision.HIGHEST)
    return smooth.reshape(R, NX, NY) * wet_mask.astype(jnp.float32)[None]
```

```python
import functools

import jax
import jax.numpy as jnp
from jax import lax
from jax.experimental import pallas as pl
from jax.experimental.pallas import tpu as pltpu
from jax.sharding import PartitionSpec as P

VMEM = pl.BlockSpec(memory_space=pltpu.VMEM)


def swap(block, bit):
    count = lax.axis_size("space")
    return lax.ppermute(block, "space", [(i, i ^ bit) for i in range(count)])


def select_kernel(position_ref, slip_ref, spread_ref):
    owners, realizations, columns = slip_ref.shape
    group = position_ref.shape[1]
    rows = spread_ref.shape[0] // realizations
    picked = jnp.zeros((realizations, group), jnp.float32)
    for owner in range(owners):
        column = lax.broadcasted_iota(jnp.int32, (columns, group), 0) + owner * columns
        chosen = jnp.where(column == position_ref[...], 1.0, 0.0).astype(jnp.bfloat16)
        picked += jnp.dot(slip_ref[owner], chosen, preferred_element_type=jnp.float32)
    source = lax.broadcasted_iota(jnp.int32, (group, group * rows), 0)
    target = lax.broadcasted_iota(jnp.int32, (group, group * rows), 1)
    repeat = jnp.where(target // rows == source, 1.0, 0.0).astype(jnp.bfloat16)
    wide = jnp.dot(picked.astype(jnp.bfloat16), repeat, preferred_element_type=jnp.float32)
    row_of = lax.broadcasted_iota(jnp.int32, wide.shape, 1) % rows
    for row in range(rows):
        spread_ref[row * realizations : (row + 1) * realizations, :] = jnp.where(
            row_of == row, wide, 0.0
        ).astype(jnp.bfloat16)


def uplift_kernel(table_ref, spread_ref, first_ref, second_ref, out_ref):
    depth = spread_ref.shape[1]
    width = first_ref.shape[2]
    both = jnp.concatenate(
        [first_ref[...].reshape(depth, width), second_ref[...].reshape(depth, width)], axis=1
    )
    value = jnp.dot(spread_ref[...], both, preferred_element_type=jnp.float32)
    for side in range(2):
        part = value[:, side * width : (side + 1) * width]
        out_ref[side] = part.reshape(out_ref.shape[1:]).astype(out_ref.dtype)


def partial_uplift(table, spread, green, rows, realizations, dtype):
    group, _, width = green.shape
    count = table.shape[0]
    return pl.pallas_call(
        uplift_kernel,
        out_shape=jax.ShapeDtypeStruct((count, rows, realizations, width), dtype),
        grid_spec=pltpu.PrefetchScalarGridSpec(
            num_scalar_prefetch=1,
            grid=(count // 2,),
            in_specs=[
                VMEM,
                pl.BlockSpec((group, rows, width), lambda i, table: (0, table[2 * i], 0)),
                pl.BlockSpec((group, rows, width), lambda i, table: (0, table[2 * i + 1], 0)),
            ],
            out_specs=pl.BlockSpec((2, rows, realizations, width), lambda i, table: (i, 0, 0, 0)),
        ),
        cost_estimate=pl.CostEstimate(
            flops=2 * count * rows * rows * realizations * group * width,
            bytes_accessed=count * rows * width * (2 * group + 4 * realizations),
            transcendentals=0,
        ),
    )(table, spread, green, green)


def bands_kernel(taps, weights_ref, bands_ref):
    half = taps // 2
    width = weights_ref.shape[1]
    source = lax.broadcasted_iota(jnp.int32, (width, width), 0)
    target = lax.broadcasted_iota(jnp.int32, (width, width), 1)
    inside = jnp.abs(source - target) <= half
    for tap in range(-1, taps + 1):
        if 0 <= tap < taps:
            line = jnp.broadcast_to(weights_ref[tap : tap + 1, :], (width, width))
            rolled = pltpu.roll(line, width - half, 1, stride=1, stride_axis=0)
            band = jnp.where(inside, rolled, 0.0).astype(jnp.bfloat16)
        else:
            band = jnp.zeros((width, width), jnp.bfloat16)
        if tap >= 0:
            bands_ref[tap * width : (tap + 1) * width, :width] = band
        if tap < taps:
            bands_ref[(tap + 1) * width : (tap + 2) * width, width:] = band


def smooth_kernel(low_ref, own_ref, high_ref, bands_ref, mask_ref, out_ref, lines_ref):
    half = low_ref.shape[0]
    rows, realizations, width = own_ref.shape

    def row_at(index):
        if index < half:
            return low_ref[index]
        if index < half + rows:
            return own_ref[index - half]
        return high_ref[index - half - rows]

    for shift in range(2 * half + 2):
        for pair in range(rows // 2):
            lines_ref[
                pair * realizations : (pair + 1) * realizations,
                shift * width : (shift + 1) * width,
            ] = row_at(2 * pair + shift)
    value = jnp.dot(lines_ref[...], bands_ref[...], preferred_element_type=jnp.float32)
    value = value.reshape(rows // 2, realizations, 2 * width)
    both = jnp.stack([value[:, :, :width], value[:, :, width:]], axis=1)
    both = both.reshape(rows, realizations, width)
    mask = mask_ref[...].astype(jnp.float32)
    out_ref[...] = jnp.transpose(both, (1, 0, 2)) * mask[None]


def reduce_halves(block, axes):
    bits = {axis: 1 << (block.ndim - 3 - axis) for axis in range(block.ndim - 3)}
    done = []
    for axis in axes:
        place = axis - sum(1 for earlier in done if earlier < axis)
        away = lax.index_in_dim(block, 1, place, keepdims=False).astype(jnp.bfloat16)
        kept = lax.index_in_dim(block, 0, place, keepdims=False)
        block = kept + swap(away, bits[axis]).astype(jnp.float32)
        done.append(axis)
    return block


def on_device(coefficients, kl_modes, green, sub_index, kernel, wet_mask):
    realizations = coefficients.shape[0]
    columns = kl_modes.shape[1]
    group, _, width = green.shape
    rows = wet_mask.shape[0]
    taps = kernel.shape[0]
    half = taps // 2
    count = lax.axis_size("space")
    me = lax.axis_index("space")
    levels = count.bit_length() - 1
    assert 1 << levels == count and half <= rows and levels >= 3

    field = jnp.dot(coefficients, kl_modes, preferred_element_type=jnp.float32)
    slip = jnp.exp(0.5 * field).astype(jnp.bfloat16)[None]
    for level in range(levels):
        slip = jnp.concatenate([slip, swap(slip, 1 << level)], axis=0)

    row_ids = lax.dynamic_slice_in_dim(sub_index, me * group, group)
    position = ((row_ids // columns) ^ me) * columns + row_ids % columns
    spread = pl.pallas_call(
        select_kernel,
        out_shape=jax.ShapeDtypeStruct((rows * realizations, group * rows), jnp.bfloat16),
        in_specs=[VMEM, VMEM],
        out_specs=VMEM,
    )(position[None], slip)

    order = 2 * jnp.arange(count // 2, dtype=jnp.int32)
    away = partial_uplift((order + 1) ^ me, spread, green, rows, realizations, jnp.bfloat16)
    kept = partial_uplift(order ^ me, spread, green, rows, realizations, jnp.float32)
    summed = kept + swap(away, 1).astype(jnp.float32)
    summed = summed.reshape((2,) * (levels - 1) + summed.shape[1:])
    below = levels - 2
    axes = list(range(below - 1, -1, -1))
    other = axes[1::-1] + axes[2:] if below >= 2 else axes
    first = reduce_halves(summed[0], axes)
    second = reduce_halves(summed[1], other)
    uplift = first + swap(second.astype(jnp.bfloat16), count // 2).astype(jnp.float32)
    seafloor = uplift.astype(jnp.bfloat16)

    low = lax.ppermute(seafloor[rows - half :], "space", [(i, i + 1) for i in range(count - 1)])
    high = lax.ppermute(seafloor[:half], "space", [(i + 1, i) for i in range(count - 1)])

    weights = (kernel / jnp.sum(kernel)).astype(jnp.bfloat16).astype(jnp.float32)
    lines = jnp.pad(weights[:, ::-1], ((0, -taps % 8), (0, width - taps)))
    bands = pl.pallas_call(
        functools.partial(bands_kernel, taps),
        out_shape=jax.ShapeDtypeStruct(((taps + 1) * width, 2 * width), jnp.bfloat16),
        in_specs=[VMEM],
        out_specs=VMEM,
    )(lines)
    return pl.pallas_call(
        smooth_kernel,
        out_shape=jax.ShapeDtypeStruct((realizations, rows, width), jnp.float32),
        in_specs=[VMEM] * 5,
        out_specs=VMEM,
        scratch_shapes=[
            pltpu.VMEM((rows // 2 * realizations, (taps + 1) * width), jnp.bfloat16)
        ],
    )(low, seafloor, high, bands, wet_mask)


def solution(mesh):
    placed = (
        P("parts", None),
        P("parts", "space"),
        P(("parts", "space"), None, None),
        P("parts"),
        P(),
        P(("parts", "space"), None),
    )
    return jax.shard_map(
        on_device, mesh=mesh, in_specs=placed, out_specs=P("parts", "space", None), check_vma=False
    )
```

```python
import functools

import jax
import jax.numpy as jnp
from jax import lax
from jax.experimental import pallas as pl
from jax.experimental.pallas import tpu as pltpu
from jax.sharding import PartitionSpec as P


VMEM = pl.BlockSpec(memory_space=pltpu.VMEM)
HBM = pl.BlockSpec(memory_space=pltpu.HBM)
PARAMS = pltpu.CompilerParams(vmem_limit_bytes=20 << 20)


def swap(block, bit):
    count = lax.axis_size("space")
    return lax.ppermute(block, "space", [(i, i ^ bit) for i in range(count)])


def slip_kernel(coefficients_ref, modes_ref, slip_ref, field_ref):
    step = pl.program_id(0)
    part = jnp.dot(coefficients_ref[...], modes_ref[...], preferred_element_type=jnp.float32)

    @pl.when(step == 0)
    def _():
        field_ref[...] = part

    @pl.when(step > 0)
    def _():
        field_ref[...] += part

    @pl.when(step == pl.num_programs(0) - 1)
    def _():
        slip_ref[0] = jnp.exp(0.5 * field_ref[...]).astype(slip_ref.dtype)


def load(green_ref, part_ref, semaphore, start):
    copy = pltpu.make_async_copy(
        green_ref.at[pl.ds(start, part_ref.shape[0])], part_ref, semaphore
    )
    copy.start()
    return copy


def choose_kernel(columns, index_ref, green_ref, part_ref, chosen_ref, semaphore):
    copy = load(green_ref, part_ref, semaphore, 0)
    me = lax.axis_index("space")
    group = index_ref.shape[1]
    row_ids = index_ref[pl.ds(me, 1), :]
    position = ((row_ids // columns) ^ me) * columns + row_ids % columns
    for start in range(0, chosen_ref.shape[0], group):
        row = lax.broadcasted_iota(jnp.int32, (group, group), 0) + start
        chosen_ref[start : start + group, :] = jnp.where(row == position, 1.0, 0.0).astype(
            jnp.bfloat16
        )
    copy.wait()


def repeat_kernel(rows, green_ref, part_ref, repeat_ref, semaphore):
    copy = load(green_ref, part_ref, semaphore, green_ref.shape[0] - part_ref.shape[0])
    source = lax.broadcasted_iota(jnp.int32, repeat_ref.shape, 0)
    target = lax.broadcasted_iota(jnp.int32, repeat_ref.shape, 1)
    near = (target >= source * rows) & (target < (source + 1) * rows)
    repeat_ref[...] = jnp.where(near, 1.0, 0.0).astype(jnp.bfloat16)
    copy.wait()


def select_kernel(chosen_ref, repeat_ref, slip_ref, spread_ref):
    owners, realizations, _ = slip_ref.shape
    rows = spread_ref.shape[0] // realizations
    slip = jnp.concatenate([slip_ref[owner] for owner in range(owners)], axis=1)
    picked = jnp.dot(slip, chosen_ref[...], preferred_element_type=jnp.float32)
    wide = jnp.dot(
        picked.astype(jnp.bfloat16), repeat_ref[...], preferred_element_type=jnp.float32
    )
    row_of = lax.broadcasted_iota(jnp.int32, wide.shape, 1) % rows
    for row in range(rows):
        spread_ref[row * realizations : (row + 1) * realizations, :] = jnp.where(
            row_of == row, wide, 0.0
        ).astype(jnp.bfloat16)


def uplift_kernel(groups, rows, spread_ref, low_ref, high_ref, *rest):
    arrived, outs = rest[: -len(groups)], rest[-len(groups) :]
    depth = low_ref.shape[0] * rows
    width = low_ref.shape[2]
    me = lax.axis_index("space")

    def block(place):
        first = pl.multiple_of((me ^ place) * rows, rows)
        parts = [
            ref[:, pl.ds(first, rows), :].reshape(depth, width) for ref in (low_ref, high_ref)
        ]
        return jnp.concatenate(parts, axis=0)

    columns = jnp.concatenate([block(place) for group in groups for place in group], axis=1)
    value = jnp.dot(spread_ref[...], columns, preferred_element_type=jnp.float32)
    side = 0
    for group, out_ref in zip(groups, outs):
        for slot in range(len(group)):
            part = value[:, side * width : (side + 1) * width].reshape(out_ref.shape[1:])
            if arrived:
                part += arrived[0][side].astype(jnp.float32)
            out_ref[slot] = part.astype(out_ref.dtype)
            side += 1


def uplift_blocks(groups, rows, realizations, dtype, spread, parts, *arrived):
    width = parts[0].shape[2]
    return pl.pallas_call(
        functools.partial(uplift_kernel, groups, rows),
        out_shape=[
            jax.ShapeDtypeStruct((len(group), rows, realizations, width), dtype)
            for group in groups
        ],
        in_specs=[VMEM] * (3 + len(arrived)),
        out_specs=[VMEM] * len(groups),
        compiler_params=PARAMS,
    )(spread, *parts, *arrived)


def bands_kernel(kernel_ref, bands_ref):
    taps = kernel_ref.shape[0]
    half = taps // 2
    width = bands_ref.shape[1] // 2
    weights = (kernel_ref[...] / jnp.sum(kernel_ref[...])).astype(jnp.bfloat16)
    first = lax.broadcasted_iota(jnp.int32, (taps, width), 0)
    second = lax.broadcasted_iota(jnp.int32, (taps, width), 1)
    mirror = jnp.where(first + second == taps - 1, 1.0, 0.0).astype(jnp.bfloat16)
    lines = jnp.dot(weights, mirror, preferred_element_type=jnp.float32)
    source = lax.broadcasted_iota(jnp.int32, (width, width), 0)
    target = lax.broadcasted_iota(jnp.int32, (width, width), 1)
    inside = jnp.abs(source - target) <= half
    for tap in range(-1, taps + 1):
        if 0 <= tap < taps:
            line = jnp.broadcast_to(lines[tap : tap + 1, :], (width, width))
            rolled = pltpu.roll(line, width - half, 1, stride=1, stride_axis=0)
            band = jnp.where(inside, rolled, 0.0).astype(jnp.bfloat16)
        else:
            band = jnp.zeros((width, width), jnp.bfloat16)
        if tap >= 0:
            bands_ref[tap * width : (tap + 1) * width, :width] = band
        if tap < taps:
            bands_ref[(tap + 1) * width : (tap + 2) * width, width:] = band


def smooth_kernel(low_ref, own_ref, high_ref, bands_ref, mask_ref, out_ref, lines_ref):
    half = low_ref.shape[0]
    rows, realizations, width = own_ref.shape

    def row_at(index):
        if index < half:
            return low_ref[index]
        if index < half + rows:
            return own_ref[index - half]
        return high_ref[index - half - rows]

    for shift in range(2 * half + 2):
        for pair in range(rows // 2):
            lines_ref[
                pair * realizations : (pair + 1) * realizations,
                shift * width : (shift + 1) * width,
            ] = row_at(2 * pair + shift)
    value = jnp.dot(lines_ref[...], bands_ref[...], preferred_element_type=jnp.float32)
    value = value.reshape(rows // 2, realizations, 2 * width)
    both = jnp.stack([value[:, :, :width], value[:, :, width:]], axis=1)
    both = both.reshape(rows, realizations, width)
    mask = mask_ref[...].astype(jnp.float32)
    out_ref[...] = jnp.transpose(both, (1, 0, 2)) * mask[None]


def reduce_halves(block, places, bits):
    for bit in bits:
        kept = [slot for slot, place in enumerate(places) if not place & bit]
        away = [slot for slot, place in enumerate(places) if place & bit]
        step = away[0] - kept[0]
        shape = (len(places) // (2 * step), 2, step)
        pairs = block.reshape(shape + block.shape[1:])
        sent = pairs[:, 1].reshape((-1,) + block.shape[1:]).astype(jnp.bfloat16)
        block = pairs[:, 0].reshape(sent.shape) + swap(sent, bit).astype(jnp.float32)
        places = [places[slot] for slot in kept]
    return block


def body(coefficients, kl_modes, green, sub_index, kernel, wet_mask):
    realizations, modes = coefficients.shape
    columns = kl_modes.shape[1]
    group, _, width = green.shape
    rows = wet_mask.shape[0]
    taps = kernel.shape[0]
    half = taps // 2
    count = lax.axis_size("space")
    levels = count.bit_length() - 1
    assert 1 << levels == count and half <= rows and levels >= 4
    green = pltpu.with_memory_space_constraint(green, pltpu.HBM)

    slip = pl.pallas_call(
        slip_kernel,
        out_shape=jax.ShapeDtypeStruct((1, realizations, columns), jnp.bfloat16),
        grid=(4,),
        in_specs=[
            pl.BlockSpec((realizations, modes // 4), lambda i: (0, i)),
            pl.BlockSpec((modes // 4, columns), lambda i: (i, 0)),
        ],
        out_specs=pl.BlockSpec((1, realizations, columns), lambda i: (0, 0, 0)),
        scratch_shapes=[pltpu.VMEM((realizations, columns), jnp.float32)],
        compiler_params=PARAMS,
    )(
        pltpu.with_memory_space_constraint(coefficients, pltpu.HBM),
        pltpu.with_memory_space_constraint(kl_modes, pltpu.HBM),
    )
    for level in range(levels):
        arrived = swap(slip, 1 << level)
        slip = jnp.concatenate([slip, arrived], axis=0)

    part = jax.ShapeDtypeStruct((group // 2,) + green.shape[1:], green.dtype)
    low, chosen = pl.pallas_call(
        functools.partial(choose_kernel, columns),
        out_shape=(part, jax.ShapeDtypeStruct((sub_index.shape[0], group), jnp.bfloat16)),
        in_specs=[VMEM, HBM],
        out_specs=(VMEM, VMEM),
        scratch_shapes=[pltpu.SemaphoreType.DMA],
        compiler_params=PARAMS,
    )(sub_index.reshape(-1, group), green)
    high, repeat = pl.pallas_call(
        functools.partial(repeat_kernel, rows),
        out_shape=(part, jax.ShapeDtypeStruct((group, group * rows), jnp.bfloat16)),
        in_specs=[HBM],
        out_specs=(VMEM, VMEM),
        scratch_shapes=[pltpu.SemaphoreType.DMA],
        compiler_params=PARAMS,
    )(green)
    bands = pl.pallas_call(
        bands_kernel,
        out_shape=jax.ShapeDtypeStruct(((taps + 1) * width, 2 * width), jnp.bfloat16),
        in_specs=[VMEM],
        out_specs=VMEM,
        compiler_params=PARAMS,
    )(kernel)

    spread = pl.pallas_call(
        select_kernel,
        out_shape=jax.ShapeDtypeStruct((rows * realizations, group * rows), jnp.bfloat16),
        in_specs=[VMEM] * 3,
        out_specs=VMEM,
        compiler_params=PARAMS,
    )(chosen, repeat, slip)

    top = count // 2
    even = list(range(0, count, 2))
    away_first = [p for p in even if p < top and p & 2]
    away_second = [p for p in even if p >= top and p & 4]
    keep_first = [p for p in even if p < top and not p & 2]
    keep_second = [p for p in even if p >= top and not p & 4]
    away = away_first + away_second
    keep = keep_first + keep_second

    def blocks(places, dtype, *arrived):
        return uplift_blocks(places, rows, realizations, dtype, spread, (low, high), *arrived)

    (to_send,) = blocks([[place | 1 for place in away]], jnp.bfloat16)
    arrived_away = swap(to_send, 1)
    (to_keep,) = blocks([[place | 1 for place in keep]], jnp.bfloat16)
    arrived_keep = swap(to_keep, 1)
    sent = blocks([away_first, away_second], jnp.bfloat16, arrived_away)
    arrived_first = swap(sent[0], 2)
    arrived_second = swap(sent[1], 4)
    kept = blocks([keep_first, keep_second], jnp.float32, arrived_keep)
    later = [8 << level for level in range(levels - 4)]
    first = reduce_halves(
        kept[0] + arrived_first.astype(jnp.float32), keep_first, [4] + later
    )
    second = reduce_halves(
        kept[1] + arrived_second.astype(jnp.float32), keep_second, [2] + later
    )
    arrived = swap(second.astype(jnp.bfloat16), top)
    seafloor = (first + arrived.astype(jnp.float32))[0].astype(jnp.bfloat16)

    low_rows = lax.ppermute(seafloor[rows - half :], "space", [(i, i + 1) for i in range(count - 1)])
    high_rows = lax.ppermute(seafloor[:half], "space", [(i + 1, i) for i in range(count - 1)])
    return pl.pallas_call(
        smooth_kernel,
        out_shape=jax.ShapeDtypeStruct((realizations, rows, width), jnp.float32),
        in_specs=[VMEM] * 5,
        out_specs=VMEM,
        scratch_shapes=[
            pltpu.VMEM((rows // 2 * realizations, (taps + 1) * width), jnp.bfloat16)
        ],
        compiler_params=PARAMS,
    )(low_rows, seafloor, high_rows, bands, wet_mask)


def solution(mesh):
    placed = (
        P("parts", None),
        P("parts", "space"),
        P(("parts", "space"), None, None),
        P("parts"),
        P(),
        P(("parts", "space"), None),
    )
    return jax.shard_map(
        body, mesh=mesh, in_specs=placed, out_specs=P("parts", "space", None), check_vma=False
    )
```

```python
import functools

import jax
import jax.numpy as jnp
from jax import lax
from jax.experimental import pallas as pl
from jax.experimental.pallas import tpu as pltpu
from jax.sharding import PartitionSpec as P


VMEM = pl.BlockSpec(memory_space=pltpu.VMEM)
HBM = pl.BlockSpec(memory_space=pltpu.HBM)
PARAMS = pltpu.CompilerParams(vmem_limit_bytes=20 << 20)


def swap(block, bit):
    count = lax.axis_size("space")
    return lax.ppermute(block, "space", [(i, i ^ bit) for i in range(count)])


def slip_kernel(coefficients_hbm, modes_hbm, slip_ref, coefficients_ref, modes_ref, semaphores):
    parts = semaphores.shape[0] - 1
    depth = modes_ref.shape[0] // parts
    first = pltpu.make_async_copy(coefficients_hbm, coefficients_ref, semaphores.at[parts])
    first.start()
    copies = []
    for part in range(parts):
        lines = pl.ds(part * depth, depth)
        copies.append(
            pltpu.make_async_copy(
                modes_hbm.at[lines], modes_ref.at[lines], semaphores.at[part]
            )
        )
        copies[part].start()
    first.wait()
    field = jnp.zeros(slip_ref.shape[1:], jnp.float32)
    for part in range(parts):
        lines = slice(part * depth, (part + 1) * depth)
        copies[part].wait()
        field += jnp.dot(
            coefficients_ref[:, lines], modes_ref[lines], preferred_element_type=jnp.float32
        )
    slip_ref[0] = jnp.exp(0.5 * field).astype(slip_ref.dtype)


def load(green_ref, part_ref, semaphore, start):
    copy = pltpu.make_async_copy(
        green_ref.at[pl.ds(start, part_ref.shape[0])], part_ref, semaphore
    )
    copy.start()
    return copy


def choose_kernel(start, columns, index_hbm, green_ref, part_ref, chosen_ref, index_ref, semaphores):
    fetch = pltpu.make_async_copy(index_hbm, index_ref, semaphores.at[0])
    fetch.start()
    copy = load(green_ref, part_ref, semaphores.at[1], start)
    me = lax.axis_index("space")
    group = index_ref.shape[1]
    fetch.wait()
    row_ids = index_ref[pl.ds(me, 1), :]
    position = ((row_ids // columns) ^ me) * columns + row_ids % columns
    for first in range(0, chosen_ref.shape[0], group):
        row = lax.broadcasted_iota(jnp.int32, (group, group), 0) + first
        chosen_ref[first : first + group, :] = jnp.where(row == position, 1.0, 0.0).astype(
            jnp.bfloat16
        )
    copy.wait()


def repeat_kernel(start, rows, green_ref, part_ref, repeat_ref, semaphore):
    copy = load(green_ref, part_ref, semaphore, start)
    source = lax.broadcasted_iota(jnp.int32, repeat_ref.shape, 0)
    target = lax.broadcasted_iota(jnp.int32, repeat_ref.shape, 1)
    near = (target >= source * rows) & (target < (source + 1) * rows)
    repeat_ref[...] = jnp.where(near, 1.0, 0.0).astype(jnp.bfloat16)
    copy.wait()


def rest_kernel(start, green_ref, part_ref, semaphore):
    load(green_ref, part_ref, semaphore, start).wait()


def select_kernel(chosen_ref, repeat_ref, slip_ref, spread_ref):
    owners, realizations, _ = slip_ref.shape
    rows = spread_ref.shape[0] // realizations
    slip = jnp.concatenate([slip_ref[owner] for owner in range(owners)], axis=1)
    picked = jnp.dot(slip, chosen_ref[...], preferred_element_type=jnp.float32)
    wide = jnp.dot(
        picked.astype(jnp.bfloat16), repeat_ref[...], preferred_element_type=jnp.float32
    )
    row_of = lax.broadcasted_iota(jnp.int32, wide.shape, 1) % rows
    for row in range(rows):
        spread_ref[row * realizations : (row + 1) * realizations, :] = jnp.where(
            row_of == row, wide, 0.0
        ).astype(jnp.bfloat16)


def uplift_kernel(groups, parts, rows, spread_ref, *refs):
    parts, arrived, outs = refs[:parts], refs[parts : -len(groups)], refs[-len(groups) :]
    width = parts[0].shape[2]
    me = lax.axis_index("space")

    def block(place):
        first = pl.multiple_of((me ^ place) * rows, rows)
        pieces = [
            ref[:, pl.ds(first, rows), :].reshape(ref.shape[0] * rows, width) for ref in parts
        ]
        return jnp.concatenate(pieces, axis=0)

    columns = jnp.concatenate([block(place) for group in groups for place in group], axis=1)
    value = jnp.dot(spread_ref[...], columns, preferred_element_type=jnp.float32)
    side = 0
    for group, out_ref in zip(groups, outs):
        for slot in range(len(group)):
            part = value[:, side * width : (side + 1) * width].reshape(out_ref.shape[1:])
            if arrived:
                part += arrived[0][side].astype(jnp.float32)
            out_ref[slot] = part.astype(out_ref.dtype)
            side += 1


def uplift_blocks(groups, rows, realizations, dtype, spread, parts, *arrived):
    width = parts[0].shape[2]
    return pl.pallas_call(
        functools.partial(uplift_kernel, groups, len(parts), rows),
        out_shape=[
            jax.ShapeDtypeStruct((len(group), rows, realizations, width), dtype)
            for group in groups
        ],
        in_specs=[VMEM] * (1 + len(parts) + len(arrived)),
        out_specs=[VMEM] * len(groups),
        compiler_params=PARAMS,
    )(spread, *parts, *arrived)


def bands_kernel(kernel_ref, bands_ref):
    taps = kernel_ref.shape[0]
    half = taps // 2
    width = bands_ref.shape[1] // 2
    weights = (kernel_ref[...] / jnp.sum(kernel_ref[...])).astype(jnp.bfloat16)
    first = lax.broadcasted_iota(jnp.int32, (taps, width), 0)
    second = lax.broadcasted_iota(jnp.int32, (taps, width), 1)
    mirror = jnp.where(first + second == taps - 1, 1.0, 0.0).astype(jnp.bfloat16)
    lines = jnp.dot(weights, mirror, preferred_element_type=jnp.float32)
    source = lax.broadcasted_iota(jnp.int32, (width, width), 0)
    target = lax.broadcasted_iota(jnp.int32, (width, width), 1)
    inside = jnp.abs(source - target) <= half
    for tap in range(-1, taps + 1):
        if 0 <= tap < taps:
            line = jnp.broadcast_to(lines[tap : tap + 1, :], (width, width))
            rolled = pltpu.roll(line, width - half, 1, stride=1, stride_axis=0)
            band = jnp.where(inside, rolled, 0.0).astype(jnp.bfloat16)
        else:
            band = jnp.zeros((width, width), jnp.bfloat16)
        if tap >= 0:
            bands_ref[tap * width : (tap + 1) * width, :width] = band
        if tap < taps:
            bands_ref[(tap + 1) * width : (tap + 2) * width, width:] = band


def smooth_kernel(low_ref, own_ref, high_ref, bands_ref, mask_ref, out_ref, lines_ref):
    half = low_ref.shape[0]
    rows, realizations, width = own_ref.shape

    def row_at(index):
        if index < half:
            return low_ref[index]
        if index < half + rows:
            return own_ref[index - half]
        return high_ref[index - half - rows]

    for shift in range(2 * half + 2):
        for pair in range(rows // 2):
            lines_ref[
                pair * realizations : (pair + 1) * realizations,
                shift * width : (shift + 1) * width,
            ] = row_at(2 * pair + shift)
    value = jnp.dot(lines_ref[...], bands_ref[...], preferred_element_type=jnp.float32)
    value = value.reshape(rows // 2, realizations, 2 * width)
    both = jnp.stack([value[:, :, :width], value[:, :, width:]], axis=1)
    both = both.reshape(rows, realizations, width)
    mask = mask_ref[...].astype(jnp.float32)
    out_ref[...] = jnp.transpose(both, (1, 0, 2)) * mask[None]


def reduce_halves(block, places, bits):
    for bit in bits:
        kept = [slot for slot, place in enumerate(places) if not place & bit]
        away = [slot for slot, place in enumerate(places) if place & bit]
        step = away[0] - kept[0]
        shape = (len(places) // (2 * step), 2, step)
        pairs = block.reshape(shape + block.shape[1:])
        sent = pairs[:, 1].reshape((-1,) + block.shape[1:]).astype(jnp.bfloat16)
        block = pairs[:, 0].reshape(sent.shape) + swap(sent, bit).astype(jnp.float32)
        places = [places[slot] for slot in kept]
    return block


def body(coefficients, kl_modes, green, sub_index, kernel, wet_mask):
    realizations, _ = coefficients.shape
    columns = kl_modes.shape[1]
    group, _, width = green.shape
    rows = wet_mask.shape[0]
    taps = kernel.shape[0]
    half = taps // 2
    count = lax.axis_size("space")
    levels = count.bit_length() - 1
    assert 1 << levels == count and half <= rows and levels >= 4
    green = pltpu.with_memory_space_constraint(green, pltpu.HBM)

    slip = pl.pallas_call(
        slip_kernel,
        out_shape=jax.ShapeDtypeStruct((1, realizations, columns), jnp.bfloat16),
        in_specs=[HBM, HBM],
        out_specs=VMEM,
        scratch_shapes=[
            pltpu.VMEM(coefficients.shape, coefficients.dtype),
            pltpu.VMEM(kl_modes.shape, kl_modes.dtype),
            pltpu.SemaphoreType.DMA((5,)),
        ],
        compiler_params=PARAMS,
    )(
        pltpu.with_memory_space_constraint(coefficients, pltpu.HBM),
        pltpu.with_memory_space_constraint(kl_modes, pltpu.HBM),
    )
    for level in range(levels):
        arrived = swap(slip, 1 << level)
        slip = jnp.concatenate([slip, arrived], axis=0)

    bounds = [0, group // 4, group * 5 // 8, group]
    shapes = [
        jax.ShapeDtypeStruct((stop - start,) + green.shape[1:], green.dtype)
        for start, stop in zip(bounds, bounds[1:])
    ]
    index = pltpu.with_memory_space_constraint(sub_index.reshape(-1, group), pltpu.HBM)
    part0, chosen = pl.pallas_call(
        functools.partial(choose_kernel, bounds[0], columns),
        out_shape=(
            shapes[0],
            jax.ShapeDtypeStruct((sub_index.shape[0], group), jnp.bfloat16),
        ),
        in_specs=[HBM, HBM],
        out_specs=(VMEM, VMEM),
        scratch_shapes=[
            pltpu.VMEM(index.shape, index.dtype),
            pltpu.SemaphoreType.DMA((2,)),
        ],
        compiler_params=PARAMS,
    )(index, green)
    part1, repeat = pl.pallas_call(
        functools.partial(repeat_kernel, bounds[1], rows),
        out_shape=(shapes[1], jax.ShapeDtypeStruct((group, group * rows), jnp.bfloat16)),
        in_specs=[HBM],
        out_specs=(VMEM, VMEM),
        scratch_shapes=[pltpu.SemaphoreType.DMA],
        compiler_params=PARAMS,
    )(green)
    part2 = pl.pallas_call(
        functools.partial(rest_kernel, bounds[2]),
        out_shape=shapes[2],
        in_specs=[HBM],
        out_specs=VMEM,
        scratch_shapes=[pltpu.SemaphoreType.DMA],
        compiler_params=PARAMS,
    )(green)
    parts = (part0, part1, part2)
    bands = pl.pallas_call(
        bands_kernel,
        out_shape=jax.ShapeDtypeStruct(((taps + 1) * width, 2 * width), jnp.bfloat16),
        in_specs=[VMEM],
        out_specs=VMEM,
        compiler_params=PARAMS,
    )(kernel)

    spread = pl.pallas_call(
        select_kernel,
        out_shape=jax.ShapeDtypeStruct((rows * realizations, group * rows), jnp.bfloat16),
        in_specs=[VMEM] * 3,
        out_specs=VMEM,
        compiler_params=PARAMS,
    )(chosen, repeat, slip)

    top = count // 2
    even = list(range(0, count, 2))
    away_first = [p for p in even if p < top and p & 2]
    away_second = [p for p in even if p >= top and p & 4]
    keep_first = [p for p in even if p < top and not p & 2]
    keep_second = [p for p in even if p >= top and not p & 4]
    keep = keep_first + keep_second

    def blocks(groups, dtype, *arrived):
        return uplift_blocks(groups, rows, realizations, dtype, spread, parts, *arrived)

    def other(places):
        return [place | 1 for place in places]

    (other_first,) = blocks([other(away_first)], jnp.bfloat16)
    arrived_first = swap(other_first, 1)
    (other_second,) = blocks([other(away_second)], jnp.bfloat16)
    arrived_second = swap(other_second, 1)
    (sent_first,) = blocks([away_first], jnp.bfloat16, arrived_first)
    arrived_first = swap(sent_first, 2)
    (sent_second,) = blocks([away_second], jnp.bfloat16, arrived_second)
    arrived_second = swap(sent_second, 4)
    (other_keep,) = blocks([other(keep)], jnp.bfloat16)
    arrived_keep = swap(other_keep, 1)
    kept = blocks([keep_first, keep_second], jnp.float32, arrived_keep)
    later = [8 << level for level in range(levels - 4)]
    first = reduce_halves(
        kept[0] + arrived_first.astype(jnp.float32), keep_first, [4] + later
    )
    second = reduce_halves(
        kept[1] + arrived_second.astype(jnp.float32), keep_second, [2] + later
    )
    arrived = swap(second.astype(jnp.bfloat16), top)
    seafloor = (first + arrived.astype(jnp.float32))[0].astype(jnp.bfloat16)

    low_rows = lax.ppermute(seafloor[rows - half :], "space", [(i, i + 1) for i in range(count - 1)])
    high_rows = lax.ppermute(seafloor[:half], "space", [(i + 1, i) for i in range(count - 1)])
    return pl.pallas_call(
        smooth_kernel,
        out_shape=jax.ShapeDtypeStruct((realizations, rows, width), jnp.float32),
        in_specs=[VMEM] * 5,
        out_specs=VMEM,
        scratch_shapes=[
            pltpu.VMEM((rows // 2 * realizations, (taps + 1) * width), jnp.bfloat16)
        ],
        compiler_params=PARAMS,
    )(low_rows, seafloor, high_rows, bands, wet_mask)


def solution(mesh):
    placed = (
        P("parts", None),
        P("parts", "space"),
        P(("parts", "space"), None, None),
        P("parts"),
        P(),
        P(("parts", "space"), None),
    )
    return jax.shard_map(
        body, mesh=mesh, in_specs=placed, out_specs=P("parts", "space", None), check_vma=False
    )
```

```python
import functools

import jax
import jax.numpy as jnp
from jax import lax
from jax.experimental import pallas as pl
from jax.experimental.pallas import tpu as pltpu
from jax.sharding import PartitionSpec as P


VMEM = pl.BlockSpec(memory_space=pltpu.VMEM)
HBM = pl.BlockSpec(memory_space=pltpu.HBM)
STREAMS = 2
PARAMS = pltpu.CompilerParams(vmem_limit_bytes=20 << 20)


def swap(block, bit, odd_bit=None):
    count = lax.axis_size("space")
    bits = (bit, bit if odd_bit is None else odd_bit)
    return lax.ppermute(block, "space", [(i, i ^ bits[i & 1]) for i in range(count)])


def slip_kernel(coefficients_hbm, modes_hbm, slip_ref, coefficients_ref, modes_ref, semaphores):
    parts = semaphores.shape[0] - 1
    depth = modes_ref.shape[0] // parts
    first = pltpu.make_async_copy(coefficients_hbm, coefficients_ref, semaphores.at[parts])
    first.start()
    copies = []
    for part in range(parts):
        lines = pl.ds(part * depth, depth)
        copies.append(
            pltpu.make_async_copy(
                modes_hbm.at[lines], modes_ref.at[lines], semaphores.at[part]
            )
        )
        copies[part].start()
    first.wait()
    field = jnp.zeros(slip_ref.shape[1:], jnp.float32)
    for part in range(parts):
        lines = slice(part * depth, (part + 1) * depth)
        copies[part].wait()
        field += jnp.dot(
            coefficients_ref[:, lines], modes_ref[lines], preferred_element_type=jnp.float32
        )
    slip_ref[0] = jnp.exp(0.5 * field).astype(slip_ref.dtype)


def load(green_ref, part_ref, semaphore, start, parity):
    copy = pltpu.make_async_copy(
        green_ref.at[pl.ds(start, part_ref.shape[0]), :, parity], part_ref, semaphore
    )
    copy.start()
    return copy


def choose_kernel(columns, index_hbm, green_ref, part_ref, chosen_ref, index_ref, semaphores):
    me = lax.axis_index("space")
    fetch = pltpu.make_async_copy(index_hbm, index_ref, semaphores.at[0])
    fetch.start()
    copy = load(green_ref, part_ref, semaphores.at[1], 0, 1 - (me & 1))
    group = index_ref.shape[1]
    fetch.wait()
    for side in range(2):
        row_ids = index_ref[pl.ds(me ^ side, 1), :]
        position = ((row_ids // columns) ^ me) * columns + row_ids % columns
        for first in range(0, chosen_ref.shape[0], group):
            row = lax.broadcasted_iota(jnp.int32, (group, group), 0) + first
            chosen_ref[first : first + group, side * group : (side + 1) * group] = jnp.where(
                row == position, 1.0, 0.0
            ).astype(jnp.bfloat16)
    copy.wait()


def repeat_kernel(start, rows, green_ref, part_ref, repeat_ref, semaphore):
    copy = load(green_ref, part_ref, semaphore, start, lax.axis_index("space") & 1)
    source = lax.broadcasted_iota(jnp.int32, repeat_ref.shape, 0)
    target = lax.broadcasted_iota(jnp.int32, repeat_ref.shape, 1)
    near = (target >= source * rows) & (target < (source + 1) * rows)
    repeat_ref[...] = jnp.where(near, 1.0, 0.0).astype(jnp.bfloat16)
    copy.wait()


def rest_kernel(start, green_ref, part_ref, semaphore):
    load(green_ref, part_ref, semaphore, start, lax.axis_index("space") & 1).wait()


def select_kernel(chosen_ref, repeat_ref, slip_ref, spread_ref):
    owners, realizations, _ = slip_ref.shape
    rows = spread_ref.shape[0] // realizations
    group, depth = repeat_ref.shape
    slip = jnp.concatenate([slip_ref[owner] for owner in range(owners)], axis=1)
    picked = jnp.dot(slip, chosen_ref[...], preferred_element_type=jnp.float32)
    picked = picked.astype(jnp.bfloat16)
    row_of = lax.broadcasted_iota(jnp.int32, (realizations, depth), 1) % rows
    for side in range(2):
        wide = jnp.dot(
            picked[:, side * group : (side + 1) * group],
            repeat_ref[...],
            preferred_element_type=jnp.float32,
        )
        for row in range(rows):
            spread_ref[
                row * realizations : (row + 1) * realizations, side * depth : (side + 1) * depth
            ] = jnp.where(row_of == row, wide, 0.0).astype(jnp.bfloat16)


def turned(place):
    return (place & ~3) | ((place & 1) << 1) | ((place >> 1) & 1)


def uplift_kernel(places, stream, spread_ref, *refs):
    parts, out_ref = refs[:-1], refs[-1]
    rows, width = parts[0].shape[2:]
    me = lax.axis_index("space")

    def block(place):
        pair = (me >> 1) ^ jnp.where((me & 1) == 0, place, turned(place))
        pieces = [ref[:, pair].reshape(ref.shape[0] * rows, width) for ref in parts]
        return jnp.concatenate(pieces, axis=0)

    columns = jnp.concatenate([block(place) for place in places], axis=1)
    depth = out_ref.shape[1] * out_ref.shape[2]
    lines = spread_ref[stream * depth : (stream + 1) * depth, :]
    value = jnp.dot(lines, columns, preferred_element_type=jnp.float32)
    for slot in range(len(places)):
        part = value[:, slot * width : (slot + 1) * width].reshape(out_ref.shape[1:])
        out_ref[slot] = part.astype(out_ref.dtype)


def uplift_blocks(places, stream, realizations, dtype, spread, parts):
    rows, width = parts[0].shape[2:]
    return pl.pallas_call(
        functools.partial(uplift_kernel, places, stream),
        out_shape=jax.ShapeDtypeStruct((len(places), rows // STREAMS, realizations, width), dtype),
        in_specs=[VMEM] * (1 + len(parts)),
        out_specs=VMEM,
        compiler_params=PARAMS,
    )(spread, *parts)


def bands_kernel(kernel_ref, bands_ref):
    taps = kernel_ref.shape[0]
    half = taps // 2
    width = bands_ref.shape[1] // 2
    weights = (kernel_ref[...] / jnp.sum(kernel_ref[...])).astype(jnp.bfloat16)
    first = lax.broadcasted_iota(jnp.int32, (taps, width), 0)
    second = lax.broadcasted_iota(jnp.int32, (taps, width), 1)
    mirror = jnp.where(first + second == taps - 1, 1.0, 0.0).astype(jnp.bfloat16)
    lines = jnp.dot(weights, mirror, preferred_element_type=jnp.float32)
    source = lax.broadcasted_iota(jnp.int32, (width, width), 0)
    target = lax.broadcasted_iota(jnp.int32, (width, width), 1)
    inside = jnp.abs(source - target) <= half
    for tap in range(-1, taps + 1):
        if 0 <= tap < taps:
            line = jnp.broadcast_to(lines[tap : tap + 1, :], (width, width))
            rolled = pltpu.roll(line, width - half, 1, stride=1, stride_axis=0)
            band = jnp.where(inside, rolled, 0.0).astype(jnp.bfloat16)
        else:
            band = jnp.zeros((width, width), jnp.bfloat16)
        if tap >= 0:
            bands_ref[tap * width : (tap + 1) * width, :width] = band
        if tap < taps:
            bands_ref[(tap + 1) * width : (tap + 2) * width, width:] = band


def smooth_kernel(beside_ref, across_ref, own_ref, bands_ref, mask_ref, out_ref, tall_ref, lines_ref):
    rows, realizations, width = own_ref.shape
    half = (tall_ref.shape[0] - rows) // 2
    odd = lax.axis_index("space") & 1
    for parity, before_ref, after_ref in ((0, across_ref, beside_ref), (1, beside_ref, across_ref)):

        @pl.when(odd == parity)
        def _():
            tall_ref[:half] = before_ref[rows - half :]
            tall_ref[half + rows :] = after_ref[:half]

    tall_ref[half : half + rows] = own_ref[...]
    for shift in range(2 * half + 2):
        for pair in range(rows // 2):
            lines_ref[
                pair * realizations : (pair + 1) * realizations,
                shift * width : (shift + 1) * width,
            ] = tall_ref[2 * pair + shift]
    value = jnp.dot(lines_ref[...], bands_ref[...], preferred_element_type=jnp.float32)
    value = value.reshape(rows // 2, realizations, 2 * width)
    both = jnp.stack([value[:, :, :width], value[:, :, width:]], axis=1)
    both = both.reshape(rows, realizations, width)
    mask = mask_ref[...].astype(jnp.float32)
    out_ref[...] = jnp.transpose(both, (1, 0, 2)) * mask[None]


def body(coefficients, kl_modes, green, sub_index, kernel, wet_mask):
    realizations, _ = coefficients.shape
    columns = kl_modes.shape[1]
    group, _, width = green.shape
    rows = wet_mask.shape[0]
    taps = kernel.shape[0]
    half = taps // 2
    count = lax.axis_size("space")
    levels = count.bit_length() - 1
    assert 1 << levels == count and half <= rows and levels >= 4
    green = green.reshape(group, count // 2, 2, rows, width)
    green = pltpu.with_memory_space_constraint(green, pltpu.HBM)

    slip = pl.pallas_call(
        slip_kernel,
        out_shape=jax.ShapeDtypeStruct((1, realizations, columns), jnp.bfloat16),
        in_specs=[HBM, HBM],
        out_specs=VMEM,
        scratch_shapes=[
            pltpu.VMEM(coefficients.shape, coefficients.dtype),
            pltpu.VMEM(kl_modes.shape, kl_modes.dtype),
            pltpu.SemaphoreType.DMA((5,)),
        ],
        compiler_params=PARAMS,
    )(
        pltpu.with_memory_space_constraint(coefficients, pltpu.HBM),
        pltpu.with_memory_space_constraint(kl_modes, pltpu.HBM),
    )
    for level in range(levels):
        arrived = swap(slip, 1 << level)
        slip = jnp.concatenate([slip, arrived], axis=0)

    def part(depth):
        return jax.ShapeDtypeStruct((depth, count // 2, rows, width), green.dtype)

    index = pltpu.with_memory_space_constraint(sub_index.reshape(-1, group), pltpu.HBM)
    away, chosen = pl.pallas_call(
        functools.partial(choose_kernel, columns),
        out_shape=(
            part(group),
            jax.ShapeDtypeStruct((sub_index.shape[0], 2 * group), jnp.bfloat16),
        ),
        in_specs=[HBM, HBM],
        out_specs=(VMEM, VMEM),
        scratch_shapes=[
            pltpu.VMEM(index.shape, index.dtype),
            pltpu.SemaphoreType.DMA((2,)),
        ],
        compiler_params=PARAMS,
    )(index, green)
    beside = swap(away, 1)
    own_low, repeat = pl.pallas_call(
        functools.partial(repeat_kernel, 0, rows),
        out_shape=(
            part(group // 2),
            jax.ShapeDtypeStruct((group, group * rows), jnp.bfloat16),
        ),
        in_specs=[HBM],
        out_specs=(VMEM, VMEM),
        scratch_shapes=[pltpu.SemaphoreType.DMA],
        compiler_params=PARAMS,
    )(green)
    own_high = pl.pallas_call(
        functools.partial(rest_kernel, group // 2),
        out_shape=part(group - group // 2),
        in_specs=[HBM],
        out_specs=VMEM,
        scratch_shapes=[pltpu.SemaphoreType.DMA],
        compiler_params=PARAMS,
    )(green)
    parts = (own_low, own_high, beside)
    bands = pl.pallas_call(
        bands_kernel,
        out_shape=jax.ShapeDtypeStruct(((taps + 1) * width, 2 * width), jnp.bfloat16),
        in_specs=[VMEM],
        out_specs=VMEM,
        compiler_params=PARAMS,
    )(kernel)

    spread = pl.pallas_call(
        select_kernel,
        out_shape=jax.ShapeDtypeStruct((rows * realizations, 2 * group * rows), jnp.bfloat16),
        in_specs=[VMEM] * 3,
        out_specs=VMEM,
        compiler_params=PARAMS,
    )(chosen, repeat, slip)

    places = list(range(count // 2))
    streams = range(STREAMS)
    arrived, kept = [], []
    for stream in streams:
        sent = uplift_blocks(places[1::2], stream, realizations, jnp.bfloat16, spread, parts)
        arrived.append(swap(sent, 2, 4))
    for stream in streams:
        block = uplift_blocks(places[::2], stream, realizations, jnp.float32, spread, parts)
        kept.append(block + arrived[stream].astype(jnp.float32))
    for level in range(2, levels):
        for stream in streams:
            pairs = kept[stream].reshape((-1, 2) + kept[stream].shape[1:])
            sent = pairs[:, 1].astype(jnp.bfloat16)
            moved = swap(sent, 4, 2) if level == 2 else swap(sent, 1 << level)
            kept[stream] = pairs[:, 0] + moved.astype(jnp.float32)
    seafloor = jnp.concatenate([block[0].astype(jnp.bfloat16) for block in kept], axis=0)

    crossing = [(i, i + 1) for i in range(1, count - 1, 2)]
    crossing += [(target, source) for source, target in crossing]
    across = lax.ppermute(seafloor, "space", crossing)
    beside = swap(seafloor, 1)
    return pl.pallas_call(
        smooth_kernel,
        out_shape=jax.ShapeDtypeStruct((realizations, rows, width), jnp.float32),
        in_specs=[VMEM] * 5,
        out_specs=VMEM,
        scratch_shapes=[
            pltpu.VMEM((rows + 2 * half, realizations, width), jnp.bfloat16),
            pltpu.VMEM((rows // 2 * realizations, (taps + 1) * width), jnp.bfloat16),
        ],
        compiler_params=PARAMS,
    )(beside, across, seafloor, bands, wet_mask)


def solution(mesh):
    placed = (
        P("parts", None),
        P("parts", "space"),
        P(("parts", "space"), None, None),
        P("parts"),
        P(),
        P(("parts", "space"), None),
    )
    return jax.shard_map(
        body, mesh=mesh, in_specs=placed, out_specs=P("parts", "space", None), check_vma=False
    )
```

```python
import functools

import jax
import jax.numpy as jnp
from jax import lax
from jax.experimental import pallas as pl
from jax.experimental.pallas import tpu as pltpu
from jax.sharding import PartitionSpec as P


VMEM = pl.BlockSpec(memory_space=pltpu.VMEM)
HBM = pl.BlockSpec(memory_space=pltpu.HBM)
STREAMS = 2
PARAMS = pltpu.CompilerParams(vmem_limit_bytes=20 << 20)


def swap(block, bit, odd_bit=None):
    count = lax.axis_size("space")
    bits = (bit, bit if odd_bit is None else odd_bit)
    return lax.ppermute(block, "space", [(i, i ^ bits[i & 1]) for i in range(count)])


def slip_kernel(coefficients_hbm, modes_hbm, slip_ref, coefficients_ref, modes_ref, semaphores):
    parts = semaphores.shape[0] - 1
    depth = modes_ref.shape[0] // parts
    first = pltpu.make_async_copy(coefficients_hbm, coefficients_ref, semaphores.at[parts])
    first.start()
    copies = []
    for part in range(parts):
        lines = pl.ds(part * depth, depth)
        copies.append(
            pltpu.make_async_copy(
                modes_hbm.at[lines], modes_ref.at[lines], semaphores.at[part]
            )
        )
        copies[part].start()
    first.wait()
    field = jnp.zeros(slip_ref.shape[1:], jnp.float32)
    for part in range(parts):
        lines = slice(part * depth, (part + 1) * depth)
        copies[part].wait()
        field += jnp.dot(
            coefficients_ref[:, lines], modes_ref[lines], preferred_element_type=jnp.float32
        )
    slip_ref[0] = jnp.exp(0.5 * field).astype(slip_ref.dtype)


def load(green_ref, part_ref, semaphore, start, parity):
    copy = pltpu.make_async_copy(
        green_ref.at[pl.ds(start, part_ref.shape[0]), :, parity], part_ref, semaphore
    )
    copy.start()
    return copy


def choose_kernel(columns, levels, index_hbm, green_ref, part_ref, chosen_ref, index_ref, semaphores):
    me = lax.axis_index("space")
    fetch = pltpu.make_async_copy(index_hbm, index_ref, semaphores.at[0])
    fetch.start()
    copy = load(green_ref, part_ref, semaphores.at[1], 0, 1 - (me & 1))
    group = index_ref.shape[1]
    fetch.wait()
    for side in range(2):
        row_ids = index_ref[pl.ds(me ^ side, 1), :]
        distance = (row_ids // columns) ^ me
        slot = (distance >> 1) | ((distance & 1) << (levels - 1))
        position = slot * columns + row_ids % columns
        for first in range(0, chosen_ref.shape[0], group):
            row = lax.broadcasted_iota(jnp.int32, (group, group), 0) + first
            chosen_ref[first : first + group, side * group : (side + 1) * group] = jnp.where(
                row == position, 1.0, 0.0
            ).astype(jnp.bfloat16)
    copy.wait()


def repeat_kernel(rows, green_ref, away_ref, own_ref, repeat_ref, semaphores):
    odd = lax.axis_index("space") & 1
    first = green_ref.shape[0] - away_ref.shape[0]
    copies = (
        load(green_ref, away_ref, semaphores.at[0], first, 1 - odd),
        load(green_ref, own_ref, semaphores.at[1], 0, odd),
    )
    source = lax.broadcasted_iota(jnp.int32, repeat_ref.shape, 0)
    target = lax.broadcasted_iota(jnp.int32, repeat_ref.shape, 1)
    near = (target >= source * rows) & (target < (source + 1) * rows)
    repeat_ref[...] = jnp.where(near, 1.0, 0.0).astype(jnp.bfloat16)
    for copy in copies:
        copy.wait()


def rest_kernel(green_ref, own_ref, semaphore):
    first = green_ref.shape[0] - own_ref.shape[0]
    load(green_ref, own_ref, semaphore, first, lax.axis_index("space") & 1).wait()


def select_kernel(rows, start, chosen_ref, repeat_ref, slip_ref, spread_ref):
    owners, realizations, _ = slip_ref.shape
    group, depth = repeat_ref.shape
    slip = jnp.concatenate([slip_ref[owner] for owner in range(owners)], axis=1)
    picked = jnp.dot(slip, chosen_ref[...], preferred_element_type=jnp.float32)
    picked = picked.astype(jnp.bfloat16)
    row_of = lax.broadcasted_iota(jnp.int32, (realizations, depth), 1) % rows
    for side in range(2):
        wide = jnp.dot(
            picked[:, side * group : (side + 1) * group],
            repeat_ref[...],
            preferred_element_type=jnp.float32,
        )
        for row in range(spread_ref.shape[0] // realizations):
            spread_ref[
                row * realizations : (row + 1) * realizations, side * depth : (side + 1) * depth
            ] = jnp.where(row_of == start + row, wide, 0.0).astype(jnp.bfloat16)


def turned(place):
    return (place & ~3) | ((place & 1) << 1) | ((place >> 1) & 1)


def uplift_kernel(places, stream, spread_ref, *refs):
    parts, out_ref = refs[:-1], refs[-1]
    rows, width = parts[0].shape[2:]
    me = lax.axis_index("space")

    def block(place):
        pair = (me >> 1) ^ jnp.where((me & 1) == stream % 2, place, turned(place))
        pieces = [ref[:, pair].reshape(ref.shape[0] * rows, width) for ref in parts]
        return jnp.concatenate(pieces, axis=0)

    columns = jnp.concatenate([block(place) for place in places], axis=1)
    value = jnp.dot(spread_ref[...], columns, preferred_element_type=jnp.float32)
    for slot in range(len(places)):
        part = value[:, slot * width : (slot + 1) * width].reshape(out_ref.shape[1:])
        out_ref[slot] = part.astype(out_ref.dtype)


def uplift_blocks(places, stream, realizations, dtype, spread, parts):
    width = parts[0].shape[3]
    lines = spread.shape[0] // realizations
    return pl.pallas_call(
        functools.partial(uplift_kernel, places, stream),
        out_shape=jax.ShapeDtypeStruct((len(places), lines, realizations, width), dtype),
        in_specs=[VMEM] * (1 + len(parts)),
        out_specs=VMEM,
        compiler_params=PARAMS,
    )(spread, *parts)


def bands_kernel(kernel_ref, bands_ref):
    taps = kernel_ref.shape[0]
    half = taps // 2
    width = bands_ref.shape[1] // 2
    weights = (kernel_ref[...] / jnp.sum(kernel_ref[...])).astype(jnp.bfloat16)
    first = lax.broadcasted_iota(jnp.int32, (taps, width), 0)
    second = lax.broadcasted_iota(jnp.int32, (taps, width), 1)
    mirror = jnp.where(first + second == taps - 1, 1.0, 0.0).astype(jnp.bfloat16)
    lines = jnp.dot(weights, mirror, preferred_element_type=jnp.float32)
    source = lax.broadcasted_iota(jnp.int32, (width, width), 0)
    target = lax.broadcasted_iota(jnp.int32, (width, width), 1)
    inside = jnp.abs(source - target) <= half
    for tap in range(-1, taps + 1):
        if 0 <= tap < taps:
            line = jnp.broadcast_to(lines[tap : tap + 1, :], (width, width))
            rolled = pltpu.roll(line, width - half, 1, stride=1, stride_axis=0)
            band = jnp.where(inside, rolled, 0.0).astype(jnp.bfloat16)
        else:
            band = jnp.zeros((width, width), jnp.bfloat16)
        if tap >= 0:
            bands_ref[tap * width : (tap + 1) * width, :width] = band
        if tap < taps:
            bands_ref[(tap + 1) * width : (tap + 2) * width, width:] = band


def smooth_kernel(
    half, bands_ref, mask_ref, beside_ref, across_ref, own_ref, out_ref, tall_ref, lines_ref
):
    rows, realizations, width = own_ref.shape
    odd = lax.axis_index("space") & 1

    for parity, before_ref, after_ref in ((0, across_ref, beside_ref), (1, beside_ref, across_ref)):

        @pl.when(odd == parity)
        def _():
            tall_ref[:rows] = before_ref[...]
            tall_ref[2 * rows :] = after_ref[...]

    tall_ref[rows : 2 * rows] = own_ref[...]
    for shift in range(2 * half + 2):
        for pair in range(rows // 2):
            lines_ref[
                pair * realizations : (pair + 1) * realizations,
                shift * width : (shift + 1) * width,
            ] = tall_ref[rows - half + 2 * pair + shift]
    value = jnp.dot(lines_ref[...], bands_ref[...], preferred_element_type=jnp.float32)
    value = value.reshape(rows // 2, realizations, 2 * width)
    both = jnp.stack([value[:, :, :width], value[:, :, width:]], axis=1)
    both = both.reshape(rows, realizations, width)
    mask = mask_ref[...].astype(jnp.float32)
    out_ref[...] = jnp.transpose(both, (1, 0, 2)) * mask[None]


def body(coefficients, kl_modes, green, sub_index, kernel, wet_mask):
    realizations, _ = coefficients.shape
    columns = kl_modes.shape[1]
    group, _, width = green.shape
    rows = wet_mask.shape[0]
    taps = kernel.shape[0]
    half = taps // 2
    count = lax.axis_size("space")
    levels = count.bit_length() - 1
    assert 1 << levels == count and half <= rows and levels >= 4
    green = green.reshape(group, count // 2, 2, rows, width)
    green = pltpu.with_memory_space_constraint(green, pltpu.HBM)

    slip = pl.pallas_call(
        slip_kernel,
        out_shape=jax.ShapeDtypeStruct((1, realizations, columns), jnp.bfloat16),
        in_specs=[HBM, HBM],
        out_specs=VMEM,
        scratch_shapes=[
            pltpu.VMEM(coefficients.shape, coefficients.dtype),
            pltpu.VMEM(kl_modes.shape, kl_modes.dtype),
            pltpu.SemaphoreType.DMA((5,)),
        ],
        compiler_params=PARAMS,
    )(
        pltpu.with_memory_space_constraint(coefficients, pltpu.HBM),
        pltpu.with_memory_space_constraint(kl_modes, pltpu.HBM),
    )
    for level in (*range(1, levels), 0):
        arrived = swap(slip, 1 << level)
        slip = jnp.concatenate([slip, arrived], axis=0)

    def part(depth):
        return jax.ShapeDtypeStruct((depth, count // 2, rows, width), green.dtype)

    index = pltpu.with_memory_space_constraint(sub_index.reshape(-1, group), pltpu.HBM)
    away_low, chosen = pl.pallas_call(
        functools.partial(choose_kernel, columns, levels),
        out_shape=(
            part(group // 2),
            jax.ShapeDtypeStruct((sub_index.shape[0], 2 * group), jnp.bfloat16),
        ),
        in_specs=[HBM, HBM],
        out_specs=(VMEM, VMEM),
        scratch_shapes=[
            pltpu.VMEM(index.shape, index.dtype),
            pltpu.SemaphoreType.DMA((2,)),
        ],
        compiler_params=PARAMS,
    )(index, green)
    beside_low = swap(away_low, 1)
    away_high, own_low, repeat = pl.pallas_call(
        functools.partial(repeat_kernel, rows),
        out_shape=(
            part(group - group // 2),
            part(group // 4),
            jax.ShapeDtypeStruct((group, group * rows), jnp.bfloat16),
        ),
        in_specs=[HBM],
        out_specs=(VMEM, VMEM, VMEM),
        scratch_shapes=[pltpu.SemaphoreType.DMA((2,))],
        compiler_params=PARAMS,
    )(green)
    beside_high = swap(away_high, 1)
    own_high = pl.pallas_call(
        rest_kernel,
        out_shape=part(group - group // 4),
        in_specs=[HBM],
        out_specs=VMEM,
        scratch_shapes=[pltpu.SemaphoreType.DMA],
        compiler_params=PARAMS,
    )(green)
    parts = (own_low, own_high, beside_low, beside_high)
    bands = pl.pallas_call(
        bands_kernel,
        out_shape=jax.ShapeDtypeStruct(((taps + 1) * width, 2 * width), jnp.bfloat16),
        in_specs=[VMEM],
        out_specs=VMEM,
        compiler_params=PARAMS,
    )(kernel)

    lines = rows // STREAMS

    def spread(stream):
        return pl.pallas_call(
            functools.partial(select_kernel, rows, stream * lines),
            out_shape=jax.ShapeDtypeStruct(
                (lines * realizations, 2 * group * rows), jnp.bfloat16
            ),
            in_specs=[VMEM] * 3,
            out_specs=VMEM,
            compiler_params=PARAMS,
        )(chosen, repeat, slip)

    places = list(range(count // 2))
    streams = range(STREAMS)
    turns = ((2, 4), (4, 2))
    spreads, arrived, kept = [], [], []
    for stream in streams:
        spreads.append(spread(stream))
        sent = uplift_blocks(
            places[1::2], stream, realizations, jnp.bfloat16, spreads[stream], parts
        )
        arrived.append(swap(sent, *turns[stream % 2]))
    for stream in streams:
        block = uplift_blocks(
            places[::2], stream, realizations, jnp.float32, spreads[stream], parts
        )
        kept.append(block + arrived[stream].astype(jnp.float32))
    for level in range(2, levels):
        for stream in streams:
            pairs = kept[stream].reshape((-1, 2) + kept[stream].shape[1:])
            sent = pairs[:, 1].astype(jnp.bfloat16)
            bits = turns[1 - stream % 2] if level == 2 else (1 << level,)
            moved = swap(sent, *bits)
            kept[stream] = pairs[:, 0] + moved.astype(jnp.float32)
    seafloor = [block[0].astype(jnp.bfloat16) for block in kept]

    crossing = [(i, i + 1) for i in range(1, count - 1, 2)]
    crossing += [(target, source) for source, target in crossing]
    seafloor = jnp.concatenate(seafloor, axis=0)
    across = lax.ppermute(seafloor, "space", crossing)
    beside = swap(seafloor, 1)
    return pl.pallas_call(
        functools.partial(smooth_kernel, half),
        out_shape=jax.ShapeDtypeStruct((realizations, rows, width), jnp.float32),
        in_specs=[VMEM] * 5,
        out_specs=VMEM,
        scratch_shapes=[
            pltpu.VMEM((3 * rows, realizations, width), jnp.bfloat16),
            pltpu.VMEM((rows // 2 * realizations, (taps + 1) * width), jnp.bfloat16),
        ],
        compiler_params=PARAMS,
    )(bands, wet_mask, beside, across, seafloor)


def solution(mesh):
    placed = (
        P("parts", None),
        P("parts", "space"),
        P(("parts", "space"), None, None),
        P("parts"),
        P(),
        P(("parts", "space"), None),
    )
    return jax.shard_map(
        body, mesh=mesh, in_specs=placed, out_specs=P("parts", "space", None), check_vma=False
    )
```

```python
import functools

import jax
import jax.numpy as jnp
from jax import lax
from jax.experimental import pallas as pl
from jax.experimental.pallas import tpu as pltpu
from jax.sharding import PartitionSpec as P


VMEM = pl.BlockSpec(memory_space=pltpu.VMEM)
HBM = pl.BlockSpec(memory_space=pltpu.HBM)
STREAMS = 2
ORDERS = (((0, 1, 2), (1, 2, 0)), ((0, 1, 2), (1, 0, 2)))
PARAMS = pltpu.CompilerParams(vmem_limit_bytes=20 << 20)


def swap(block, bit, odd_bit=None):
    count = lax.axis_size("space")
    bits = (bit, bit if odd_bit is None else odd_bit)
    return lax.ppermute(block, "space", [(i, i ^ bits[i & 1]) for i in range(count)])


def slip_kernel(coefficients_hbm, modes_hbm, slip_ref, coefficients_ref, modes_ref, semaphores):
    parts = semaphores.shape[0] - 1
    depth = modes_ref.shape[0] // parts
    first = pltpu.make_async_copy(coefficients_hbm, coefficients_ref, semaphores.at[parts])
    first.start()
    copies = []
    for part in range(parts):
        lines = pl.ds(part * depth, depth)
        copies.append(
            pltpu.make_async_copy(
                modes_hbm.at[lines], modes_ref.at[lines], semaphores.at[part]
            )
        )
        copies[part].start()
    first.wait()
    field = jnp.zeros(slip_ref.shape[1:], jnp.float32)
    for part in range(parts):
        lines = slice(part * depth, (part + 1) * depth)
        copies[part].wait()
        field += jnp.dot(
            coefficients_ref[:, lines], modes_ref[lines], preferred_element_type=jnp.float32
        )
    slip_ref[0] = jnp.exp(0.5 * field).astype(slip_ref.dtype)


def load(green_ref, part_ref, semaphore, start, parity):
    copy = pltpu.make_async_copy(
        green_ref.at[pl.ds(start, part_ref.shape[0]), :, parity], part_ref, semaphore
    )
    copy.start()
    return copy


def choose_kernel(columns, levels, index_hbm, green_ref, part_ref, chosen_ref, index_ref, semaphores):
    me = lax.axis_index("space")
    fetch = pltpu.make_async_copy(index_hbm, index_ref, semaphores.at[0])
    fetch.start()
    copy = load(green_ref, part_ref, semaphores.at[1], 0, 1 - (me & 1))
    group = index_ref.shape[1]
    fetch.wait()
    for side in range(2):
        row_ids = index_ref[pl.ds(me ^ side, 1), :]
        distance = (row_ids // columns) ^ me
        slot = (distance >> 1) | ((distance & 1) << (levels - 1))
        position = slot * columns + row_ids % columns
        for first in range(0, chosen_ref.shape[0], group):
            row = lax.broadcasted_iota(jnp.int32, (group, group), 0) + first
            chosen_ref[first : first + group, side * group : (side + 1) * group] = jnp.where(
                row == position, 1.0, 0.0
            ).astype(jnp.bfloat16)
    copy.wait()


def repeat_kernel(rows, green_ref, away_ref, own_ref, repeat_ref, semaphores):
    odd = lax.axis_index("space") & 1
    first = green_ref.shape[0] - away_ref.shape[0]
    copies = (
        load(green_ref, away_ref, semaphores.at[0], first, 1 - odd),
        load(green_ref, own_ref, semaphores.at[1], 0, odd),
    )
    source = lax.broadcasted_iota(jnp.int32, repeat_ref.shape, 0)
    target = lax.broadcasted_iota(jnp.int32, repeat_ref.shape, 1)
    near = (target >= source * rows) & (target < (source + 1) * rows)
    repeat_ref[...] = jnp.where(near, 1.0, 0.0).astype(jnp.bfloat16)
    for copy in copies:
        copy.wait()


def rest_kernel(green_ref, own_ref, semaphore):
    first = green_ref.shape[0] - own_ref.shape[0]
    load(green_ref, own_ref, semaphore, first, lax.axis_index("space") & 1).wait()


def fill_spread(rows, start, chosen_ref, repeat_ref, slip_ref, spread_ref):
    owners, realizations, _ = slip_ref.shape
    group, depth = repeat_ref.shape
    slip = jnp.concatenate([slip_ref[owner] for owner in range(owners)], axis=1)
    picked = jnp.dot(slip, chosen_ref[...], preferred_element_type=jnp.float32)
    picked = picked.astype(jnp.bfloat16)
    row_of = lax.broadcasted_iota(jnp.int32, (realizations, depth), 1) % rows
    for side in range(2):
        wide = jnp.dot(
            picked[:, side * group : (side + 1) * group],
            repeat_ref[...],
            preferred_element_type=jnp.float32,
        )
        for row in range(spread_ref.shape[0] // realizations):
            spread_ref[
                row * realizations : (row + 1) * realizations, side * depth : (side + 1) * depth
            ] = jnp.where(row_of == start + row, wide, 0.0).astype(jnp.bfloat16)


def away_kernel(places, stream, rows, start, chosen_ref, repeat_ref, slip_ref, *refs):
    fill_spread(rows, start, chosen_ref, repeat_ref, slip_ref, refs[-1])
    uplift_kernel(places, stream, refs[-1], *refs[:-1])


def stage_bits(stream, odd, count):
    leading = ORDERS[stream][odd]
    return leading + tuple(range(len(leading), count))


def spread_bits(place, bits):
    return sum(((place >> stage) & 1) << bit for stage, bit in enumerate(bits))


def uplift_kernel(places, stream, spread_ref, *refs):
    parts, out_ref = refs[:-1], refs[-1]
    rows, width = parts[0].shape[2:]
    me = lax.axis_index("space")
    levels = parts[0].shape[1].bit_length() - 1
    even, odd = (stage_bits(stream, side, levels) for side in range(2))

    def block(place):
        pair = (me >> 1) ^ jnp.where(
            (me & 1) == 0, spread_bits(place, even), spread_bits(place, odd)
        )
        pieces = [ref[:, pair].reshape(ref.shape[0] * rows, width) for ref in parts]
        return jnp.concatenate(pieces, axis=0)

    columns = jnp.concatenate([block(place) for place in places], axis=1)
    value = jnp.dot(spread_ref[...], columns, preferred_element_type=jnp.float32)
    for slot in range(len(places)):
        part = value[:, slot * width : (slot + 1) * width].reshape(out_ref.shape[1:])
        out_ref[slot] = part.astype(out_ref.dtype)


def uplift_blocks(places, stream, realizations, dtype, spread, parts):
    width = parts[0].shape[3]
    lines = spread.shape[0] // realizations
    return pl.pallas_call(
        functools.partial(uplift_kernel, places, stream),
        out_shape=jax.ShapeDtypeStruct((len(places), lines, realizations, width), dtype),
        in_specs=[VMEM] * (1 + len(parts)),
        out_specs=VMEM,
        compiler_params=PARAMS,
    )(spread, *parts)


def bands_kernel(kernel_ref, bands_ref):
    taps = kernel_ref.shape[0]
    half = taps // 2
    width = bands_ref.shape[1] // 2
    weights = (kernel_ref[...] / jnp.sum(kernel_ref[...])).astype(jnp.bfloat16)
    first = lax.broadcasted_iota(jnp.int32, (taps, width), 0)
    second = lax.broadcasted_iota(jnp.int32, (taps, width), 1)
    mirror = jnp.where(first + second == taps - 1, 1.0, 0.0).astype(jnp.bfloat16)
    lines = jnp.dot(weights, mirror, preferred_element_type=jnp.float32)
    source = lax.broadcasted_iota(jnp.int32, (width, width), 0)
    target = lax.broadcasted_iota(jnp.int32, (width, width), 1)
    inside = jnp.abs(source - target) <= half
    for tap in range(-1, taps + 1):
        if 0 <= tap < taps:
            line = jnp.broadcast_to(lines[tap : tap + 1, :], (width, width))
            rolled = pltpu.roll(line, width - half, 1, stride=1, stride_axis=0)
            band = jnp.where(inside, rolled, 0.0).astype(jnp.bfloat16)
        else:
            band = jnp.zeros((width, width), jnp.bfloat16)
        if tap >= 0:
            bands_ref[tap * width : (tap + 1) * width, :width] = band
        if tap < taps:
            bands_ref[(tap + 1) * width : (tap + 2) * width, width:] = band


def smooth_kernel(half, bands_ref, mask_ref, beside_ref, across_ref, own_ref, out_ref, pairs_ref):
    rows, realizations, width = own_ref.shape
    odd = lax.axis_index("space") & 1

    def place(ref, first, start, count):
        for row in range(count):
            pair, side = divmod(start + row, 2)
            pairs_ref[
                pair * realizations : (pair + 1) * realizations,
                side * width : (side + 1) * width,
            ] = ref[first + row]

    for parity, before_ref, after_ref in ((0, across_ref, beside_ref), (1, beside_ref, across_ref)):

        @pl.when(odd == parity)
        def _():
            place(before_ref, rows - half, 0, half)
            place(after_ref, 0, half + rows, half)

    place(own_ref, 0, half, rows)
    depth = rows // 2 * realizations
    lines = jnp.concatenate(
        [
            pairs_ref[shift * realizations : shift * realizations + depth, :]
            for shift in range(half + 1)
        ],
        axis=1,
    )
    value = jnp.dot(lines, bands_ref[...], preferred_element_type=jnp.float32)
    value = value.reshape(rows // 2, realizations, 2 * width)
    both = jnp.stack([value[:, :, :width], value[:, :, width:]], axis=1)
    both = both.reshape(rows, realizations, width)
    mask = mask_ref[...].astype(jnp.float32)
    out_ref[...] = jnp.transpose(both, (1, 0, 2)) * mask[None]


def body(coefficients, kl_modes, green, sub_index, kernel, wet_mask):
    realizations, _ = coefficients.shape
    columns = kl_modes.shape[1]
    group, _, width = green.shape
    rows = wet_mask.shape[0]
    taps = kernel.shape[0]
    half = taps // 2
    count = lax.axis_size("space")
    levels = count.bit_length() - 1
    assert 1 << levels == count and half <= rows and levels >= 4
    green = green.reshape(group, count // 2, 2, rows, width)
    green = pltpu.with_memory_space_constraint(green, pltpu.HBM)

    slip = pl.pallas_call(
        slip_kernel,
        out_shape=jax.ShapeDtypeStruct((1, realizations, columns), jnp.bfloat16),
        in_specs=[HBM, HBM],
        out_specs=VMEM,
        scratch_shapes=[
            pltpu.VMEM(coefficients.shape, coefficients.dtype),
            pltpu.VMEM(kl_modes.shape, kl_modes.dtype),
            pltpu.SemaphoreType.DMA((3,)),
        ],
        compiler_params=PARAMS,
    )(
        pltpu.with_memory_space_constraint(coefficients, pltpu.HBM),
        pltpu.with_memory_space_constraint(kl_modes, pltpu.HBM),
    )
    for level in (*range(1, levels), 0):
        arrived = swap(slip, 1 << level)
        slip = jnp.concatenate([slip, arrived], axis=0)

    def part(depth):
        return jax.ShapeDtypeStruct((depth, count // 2, rows, width), green.dtype)

    index = pltpu.with_memory_space_constraint(sub_index.reshape(-1, group), pltpu.HBM)
    away_low, chosen = pl.pallas_call(
        functools.partial(choose_kernel, columns, levels),
        out_shape=(
            part(group // 2),
            jax.ShapeDtypeStruct((sub_index.shape[0], 2 * group), jnp.bfloat16),
        ),
        in_specs=[HBM, HBM],
        out_specs=(VMEM, VMEM),
        scratch_shapes=[
            pltpu.VMEM(index.shape, index.dtype),
            pltpu.SemaphoreType.DMA((2,)),
        ],
        compiler_params=PARAMS,
    )(index, green)
    beside_low = swap(away_low, 1)
    away_high, own_low, repeat = pl.pallas_call(
        functools.partial(repeat_kernel, rows),
        out_shape=(
            part(group - group // 2),
            part(group // 4),
            jax.ShapeDtypeStruct((group, group * rows), jnp.bfloat16),
        ),
        in_specs=[HBM],
        out_specs=(VMEM, VMEM, VMEM),
        scratch_shapes=[pltpu.SemaphoreType.DMA((2,))],
        compiler_params=PARAMS,
    )(green)
    beside_high = swap(away_high, 1)
    own_high = pl.pallas_call(
        rest_kernel,
        out_shape=part(group - group // 4),
        in_specs=[HBM],
        out_specs=VMEM,
        scratch_shapes=[pltpu.SemaphoreType.DMA],
        compiler_params=PARAMS,
    )(green)
    parts = (own_low, own_high, beside_low, beside_high)
    bands = pl.pallas_call(
        bands_kernel,
        out_shape=jax.ShapeDtypeStruct(((taps + 1) * width, 2 * width), jnp.bfloat16),
        in_specs=[VMEM],
        out_specs=VMEM,
        compiler_params=PARAMS,
    )(kernel)

    lines = rows // STREAMS

    def away_blocks(stream):
        size = lines * realizations
        return pl.pallas_call(
            functools.partial(away_kernel, places[1::2], stream, rows, stream * lines),
            out_shape=(
                jax.ShapeDtypeStruct((count // 4, lines, realizations, width), jnp.bfloat16),
                jax.ShapeDtypeStruct((size, 2 * group * rows), jnp.bfloat16),
            ),
            in_specs=[VMEM] * (3 + len(parts)),
            out_specs=(VMEM, VMEM),
            compiler_params=PARAMS,
        )(chosen, repeat, slip, *parts)

    places = list(range(count // 2))
    streams = range(STREAMS)

    def stage_swap(block, stream, stage):
        even, odd = (stage_bits(stream, side, levels - 1)[stage] for side in range(2))
        return swap(block, 2 << even, 2 << odd)

    spreads, arrived, kept = [], [], []
    for stream in streams:
        sent, spread = away_blocks(stream)
        spreads.append(spread)
        arrived.append(stage_swap(sent, stream, 0))
    for stream in streams:
        block = uplift_blocks(
            places[::2], stream, realizations, jnp.float32, spreads[stream], parts
        )
        kept.append(block + arrived[stream].astype(jnp.float32))
    for level in range(2, levels):
        for stream in streams:
            pairs = kept[stream].reshape((-1, 2) + kept[stream].shape[1:])
            sent = pairs[:, 1].astype(jnp.bfloat16)
            moved = stage_swap(sent, stream, level - 1)
            kept[stream] = pairs[:, 0] + moved.astype(jnp.float32)
    seafloor = [block[0].astype(jnp.bfloat16) for block in kept]

    crossing = [(i, i + 1) for i in range(1, count - 1, 2)]
    crossing += [(target, source) for source, target in crossing]
    seafloor = jnp.concatenate(seafloor, axis=0)
    across = lax.ppermute(seafloor, "space", crossing)
    beside = swap(seafloor, 1)
    return pl.pallas_call(
        functools.partial(smooth_kernel, half),
        out_shape=jax.ShapeDtypeStruct((realizations, rows, width), jnp.float32),
        in_specs=[VMEM] * 5,
        out_specs=VMEM,
        scratch_shapes=[
            pltpu.VMEM(((rows // 2 + half) * realizations, 2 * width), jnp.bfloat16),
        ],
        compiler_params=PARAMS,
    )(bands, wet_mask, beside, across, seafloor)


def solution(mesh):
    placed = (
        P("parts", None),
        P("parts", "space"),
        P(("parts", "space"), None, None),
        P("parts"),
        P(),
        P(("parts", "space"), None),
    )
    return jax.shard_map(
        body, mesh=mesh, in_specs=placed, out_specs=P("parts", "space", None), check_vma=False
    )
```

```python
import functools

import jax
import jax.numpy as jnp
from jax import lax
from jax.experimental import pallas as pl
from jax.experimental.pallas import tpu as pltpu
from jax.sharding import PartitionSpec as P


VMEM = pl.BlockSpec(memory_space=pltpu.VMEM)
HBM = pl.BlockSpec(memory_space=pltpu.HBM)
STREAMS = 2
ORDERS = (((0, 1, 2), (1, 2, 0)), ((0, 1, 2), (1, 0, 2)))
PARAMS = pltpu.CompilerParams(vmem_limit_bytes=20 << 20)


def swap(block, bit, odd_bit=None):
    count = lax.axis_size("space")
    bits = (bit, bit if odd_bit is None else odd_bit)
    return lax.ppermute(block, "space", [(i, i ^ bits[i & 1]) for i in range(count)])


def slip_kernel(coefficients_hbm, modes_hbm, slip_ref, coefficients_ref, modes_ref, semaphores):
    parts = semaphores.shape[0] - 1
    depth = modes_ref.shape[0] // parts
    first = pltpu.make_async_copy(coefficients_hbm, coefficients_ref, semaphores.at[parts])
    first.start()
    copies = []
    for part in range(parts):
        lines = pl.ds(part * depth, depth)
        copies.append(
            pltpu.make_async_copy(
                modes_hbm.at[lines], modes_ref.at[lines], semaphores.at[part]
            )
        )
        copies[part].start()
    first.wait()
    field = jnp.zeros(slip_ref.shape[1:], jnp.float32)
    for part in range(parts):
        lines = slice(part * depth, (part + 1) * depth)
        copies[part].wait()
        field += jnp.dot(
            coefficients_ref[:, lines], modes_ref[lines], preferred_element_type=jnp.float32
        )
    slip_ref[0] = jnp.exp(0.5 * field).astype(slip_ref.dtype)


def load(green_ref, part_ref, semaphore, start, parity):
    copy = pltpu.make_async_copy(
        green_ref.at[pl.ds(start, part_ref.shape[0]), :, parity], part_ref, semaphore
    )
    copy.start()
    return copy


def choose_kernel(columns, levels, index_hbm, green_ref, part_ref, chosen_ref, index_ref, semaphores):
    me = lax.axis_index("space")
    fetch = pltpu.make_async_copy(index_hbm, index_ref, semaphores.at[0])
    fetch.start()
    copy = load(green_ref, part_ref, semaphores.at[1], 0, 1 - (me & 1))
    group = index_ref.shape[1]
    fetch.wait()
    for side in range(2):
        row_ids = index_ref[pl.ds(me ^ side, 1), :]
        distance = (row_ids // columns) ^ me
        slot = (distance >> 1) | ((distance & 1) << (levels - 1))
        position = slot * columns + row_ids % columns
        for first in range(0, chosen_ref.shape[0], group):
            row = lax.broadcasted_iota(jnp.int32, (group, group), 0) + first
            chosen_ref[first : first + group, side * group : (side + 1) * group] = jnp.where(
                row == position, 1.0, 0.0
            ).astype(jnp.bfloat16)
    copy.wait()


def repeat_kernel(rows, green_ref, away_ref, own_ref, repeat_ref, semaphores):
    odd = lax.axis_index("space") & 1
    first = green_ref.shape[0] - away_ref.shape[0]
    copies = (
        load(green_ref, away_ref, semaphores.at[0], first, 1 - odd),
        load(green_ref, own_ref, semaphores.at[1], 0, odd),
    )
    source = lax.broadcasted_iota(jnp.int32, repeat_ref.shape, 0)
    target = lax.broadcasted_iota(jnp.int32, repeat_ref.shape, 1)
    near = (target >= source * rows) & (target < (source + 1) * rows)
    repeat_ref[...] = jnp.where(near, 1.0, 0.0).astype(jnp.bfloat16)
    for copy in copies:
        copy.wait()


def rest_kernel(green_ref, own_ref, semaphore):
    first = green_ref.shape[0] - own_ref.shape[0]
    load(green_ref, own_ref, semaphore, first, lax.axis_index("space") & 1).wait()


def widen(chosen_ref, repeat_ref, slip_ref, wide_ref):
    group, depth = repeat_ref.shape
    slip = jnp.concatenate([slip_ref[owner] for owner in range(slip_ref.shape[0])], axis=1)
    picked = jnp.dot(slip, chosen_ref[...], preferred_element_type=jnp.float32)
    picked = picked.astype(jnp.bfloat16)
    for side in range(2):
        wide_ref[:, side * depth : (side + 1) * depth] = jnp.dot(
            picked[:, side * group : (side + 1) * group],
            repeat_ref[...],
            preferred_element_type=jnp.float32,
        )


def fill_spread(rows, start, wide_ref, spread_ref):
    realizations, depth = wide_ref.shape
    wide = wide_ref[...]
    row_of = lax.broadcasted_iota(jnp.int32, (realizations, depth), 1) % rows
    for row in range(spread_ref.shape[0] // realizations):
        spread_ref[row * realizations : (row + 1) * realizations, :] = jnp.where(
            row_of == start + row, wide, 0.0
        ).astype(jnp.bfloat16)


def first_kernel(places, rows, chosen_ref, repeat_ref, slip_ref, *refs):
    parts, (out_ref, spread_ref, wide_ref) = refs[:-3], refs[-3:]
    widen(chosen_ref, repeat_ref, slip_ref, wide_ref)
    fill_spread(rows, 0, wide_ref, spread_ref)
    uplift_kernel(places, 0, spread_ref, *parts, out_ref)


def next_kernel(places, stream, rows, start, wide_ref, *refs):
    fill_spread(rows, start, wide_ref, refs[-1])
    uplift_kernel(places, stream, refs[-1], *refs[:-1])


def stage_bits(stream, odd, count):
    leading = ORDERS[stream][odd]
    return leading + tuple(range(len(leading), count))


def spread_bits(place, bits):
    return sum(((place >> stage) & 1) << bit for stage, bit in enumerate(bits))


def uplift_kernel(places, stream, spread_ref, *refs):
    parts, out_ref = refs[:-1], refs[-1]
    rows, width = parts[0].shape[2:]
    me = lax.axis_index("space")
    levels = parts[0].shape[1].bit_length() - 1
    even, odd = (stage_bits(stream, side, levels) for side in range(2))

    def block(place):
        pair = (me >> 1) ^ jnp.where(
            (me & 1) == 0, spread_bits(place, even), spread_bits(place, odd)
        )
        pieces = [ref[:, pair].reshape(ref.shape[0] * rows, width) for ref in parts]
        return jnp.concatenate(pieces, axis=0)

    columns = jnp.concatenate([block(place) for place in places], axis=1)
    value = jnp.dot(spread_ref[...], columns, preferred_element_type=jnp.float32)
    for slot in range(len(places)):
        part = value[:, slot * width : (slot + 1) * width].reshape(out_ref.shape[1:])
        out_ref[slot] = part.astype(out_ref.dtype)


def uplift_blocks(places, stream, realizations, dtype, spread, parts):
    width = parts[0].shape[3]
    lines = spread.shape[0] // realizations
    return pl.pallas_call(
        functools.partial(uplift_kernel, places, stream),
        out_shape=jax.ShapeDtypeStruct((len(places), lines, realizations, width), dtype),
        in_specs=[VMEM] * (1 + len(parts)),
        out_specs=VMEM,
        compiler_params=PARAMS,
    )(spread, *parts)


def bands_kernel(kernel_ref, bands_ref):
    taps = kernel_ref.shape[0]
    half = taps // 2
    width = bands_ref.shape[1] // 2
    weights = (kernel_ref[...] / jnp.sum(kernel_ref[...])).astype(jnp.bfloat16)
    first = lax.broadcasted_iota(jnp.int32, (taps, width), 0)
    second = lax.broadcasted_iota(jnp.int32, (taps, width), 1)
    mirror = jnp.where(first + second == taps - 1, 1.0, 0.0).astype(jnp.bfloat16)
    lines = jnp.dot(weights, mirror, preferred_element_type=jnp.float32)
    source = lax.broadcasted_iota(jnp.int32, (width, width), 0)
    target = lax.broadcasted_iota(jnp.int32, (width, width), 1)
    inside = jnp.abs(source - target) <= half
    for tap in range(-1, taps + 1):
        if 0 <= tap < taps:
            line = jnp.broadcast_to(lines[tap : tap + 1, :], (width, width))
            rolled = pltpu.roll(line, width - half, 1, stride=1, stride_axis=0)
            band = jnp.where(inside, rolled, 0.0).astype(jnp.bfloat16)
        else:
            band = jnp.zeros((width, width), jnp.bfloat16)
        if tap >= 0:
            bands_ref[tap * width : (tap + 1) * width, :width] = band
        if tap < taps:
            bands_ref[(tap + 1) * width : (tap + 2) * width, width:] = band


def smooth_kernel(half, bands_ref, mask_ref, beside_ref, across_ref, own_ref, out_ref, pairs_ref):
    rows, realizations, width = own_ref.shape
    odd = lax.axis_index("space") & 1

    def place(ref, first, start, count):
        for row in range(count):
            pair, side = divmod(start + row, 2)
            pairs_ref[
                pair * realizations : (pair + 1) * realizations,
                side * width : (side + 1) * width,
            ] = ref[first + row]

    for parity, before_ref, after_ref in ((0, across_ref, beside_ref), (1, beside_ref, across_ref)):

        @pl.when(odd == parity)
        def _():
            place(before_ref, rows - half, 0, half)
            place(after_ref, 0, half + rows, half)

    place(own_ref, 0, half, rows)
    depth = rows // 2 * realizations
    lines = jnp.concatenate(
        [
            pairs_ref[shift * realizations : shift * realizations + depth, :]
            for shift in range(half + 1)
        ],
        axis=1,
    )
    value = jnp.dot(lines, bands_ref[...], preferred_element_type=jnp.float32)
    value = value.reshape(rows // 2, realizations, 2 * width)
    both = jnp.stack([value[:, :, :width], value[:, :, width:]], axis=1)
    both = both.reshape(rows, realizations, width)
    mask = mask_ref[...].astype(jnp.float32)
    out_ref[...] = jnp.transpose(both, (1, 0, 2)) * mask[None]


def body(coefficients, kl_modes, green, sub_index, kernel, wet_mask):
    realizations, _ = coefficients.shape
    columns = kl_modes.shape[1]
    group, _, width = green.shape
    rows = wet_mask.shape[0]
    taps = kernel.shape[0]
    half = taps // 2
    count = lax.axis_size("space")
    levels = count.bit_length() - 1
    assert 1 << levels == count and half <= rows and levels >= 4
    green = green.reshape(group, count // 2, 2, rows, width)
    green = pltpu.with_memory_space_constraint(green, pltpu.HBM)

    slip = pl.pallas_call(
        slip_kernel,
        out_shape=jax.ShapeDtypeStruct((1, realizations, columns), jnp.bfloat16),
        in_specs=[HBM, HBM],
        out_specs=VMEM,
        scratch_shapes=[
            pltpu.VMEM(coefficients.shape, coefficients.dtype),
            pltpu.VMEM(kl_modes.shape, kl_modes.dtype),
            pltpu.SemaphoreType.DMA((3,)),
        ],
        compiler_params=PARAMS,
    )(
        pltpu.with_memory_space_constraint(coefficients, pltpu.HBM),
        pltpu.with_memory_space_constraint(kl_modes, pltpu.HBM),
    )
    for level in (*range(1, levels), 0):
        arrived = swap(slip, 1 << level)
        slip = jnp.concatenate([slip, arrived], axis=0)

    def part(depth):
        return jax.ShapeDtypeStruct((depth, count // 2, rows, width), green.dtype)

    index = pltpu.with_memory_space_constraint(sub_index.reshape(-1, group), pltpu.HBM)
    away_low, chosen = pl.pallas_call(
        functools.partial(choose_kernel, columns, levels),
        out_shape=(
            part(group // 2),
            jax.ShapeDtypeStruct((sub_index.shape[0], 2 * group), jnp.bfloat16),
        ),
        in_specs=[HBM, HBM],
        out_specs=(VMEM, VMEM),
        scratch_shapes=[
            pltpu.VMEM(index.shape, index.dtype),
            pltpu.SemaphoreType.DMA((2,)),
        ],
        compiler_params=PARAMS,
    )(index, green)
    beside_low = swap(away_low, 1)
    away_high, own_low, repeat = pl.pallas_call(
        functools.partial(repeat_kernel, rows),
        out_shape=(
            part(group - group // 2),
            part(group // 4),
            jax.ShapeDtypeStruct((group, group * rows), jnp.bfloat16),
        ),
        in_specs=[HBM],
        out_specs=(VMEM, VMEM, VMEM),
        scratch_shapes=[pltpu.SemaphoreType.DMA((2,))],
        compiler_params=PARAMS,
    )(green)
    beside_high = swap(away_high, 1)
    own_high = pl.pallas_call(
        rest_kernel,
        out_shape=part(group - group // 4),
        in_specs=[HBM],
        out_specs=VMEM,
        scratch_shapes=[pltpu.SemaphoreType.DMA],
        compiler_params=PARAMS,
    )(green)
    parts = (own_low, own_high, beside_low, beside_high)
    bands = pl.pallas_call(
        bands_kernel,
        out_shape=jax.ShapeDtypeStruct(((taps + 1) * width, 2 * width), jnp.bfloat16),
        in_specs=[VMEM],
        out_specs=VMEM,
        compiler_params=PARAMS,
    )(kernel)

    lines = rows // STREAMS

    wide = []

    def away_blocks(stream):
        sides = 2 * group * rows
        shapes = (
            jax.ShapeDtypeStruct((count // 4, lines, realizations, width), jnp.bfloat16),
            jax.ShapeDtypeStruct((lines * realizations, sides), jnp.bfloat16),
        )
        if stream == 0:
            sent, spread, table = pl.pallas_call(
                functools.partial(first_kernel, places[1::2], rows),
                out_shape=(*shapes, jax.ShapeDtypeStruct((realizations, sides), jnp.float32)),
                in_specs=[VMEM] * (3 + len(parts)),
                out_specs=(VMEM, VMEM, VMEM),
                compiler_params=PARAMS,
            )(chosen, repeat, slip, *parts)
            wide.append(table)
            return sent, spread
        return pl.pallas_call(
            functools.partial(next_kernel, places[1::2], stream, rows, stream * lines),
            out_shape=shapes,
            in_specs=[VMEM] * (1 + len(parts)),
            out_specs=(VMEM, VMEM),
            compiler_params=PARAMS,
        )(wide[0], *parts)

    places = list(range(count // 2))
    streams = range(STREAMS)

    def stage_swap(block, stream, stage):
        even, odd = (stage_bits(stream, side, levels - 1)[stage] for side in range(2))
        return swap(block, 2 << even, 2 << odd)

    spreads, arrived, kept = [], [], []
    for stream in streams:
        sent, spread = away_blocks(stream)
        spreads.append(spread)
        arrived.append(stage_swap(sent, stream, 0))
    for stream in streams:
        block = uplift_blocks(
            places[::2], stream, realizations, jnp.float32, spreads[stream], parts
        )
        kept.append(block + arrived[stream].astype(jnp.float32))
    for level in range(2, levels):
        for stream in streams:
            pairs = kept[stream].reshape((-1, 2) + kept[stream].shape[1:])
            sent = pairs[:, 1].astype(jnp.bfloat16)
            moved = stage_swap(sent, stream, level - 1)
            kept[stream] = pairs[:, 0] + moved.astype(jnp.float32)
    seafloor = [block[0].astype(jnp.bfloat16) for block in kept]

    crossing = [(i, i + 1) for i in range(1, count - 1, 2)]
    crossing += [(target, source) for source, target in crossing]
    seafloor = jnp.concatenate(seafloor, axis=0)
    across = lax.ppermute(seafloor, "space", crossing)
    beside = swap(seafloor, 1)
    return pl.pallas_call(
        functools.partial(smooth_kernel, half),
        out_shape=jax.ShapeDtypeStruct((realizations, rows, width), jnp.float32),
        in_specs=[VMEM] * 5,
        out_specs=VMEM,
        scratch_shapes=[
            pltpu.VMEM(((rows // 2 + half) * realizations, 2 * width), jnp.bfloat16),
        ],
        compiler_params=PARAMS,
    )(bands, wet_mask, beside, across, seafloor)


def solution(mesh):
    placed = (
        P("parts", None),
        P("parts", "space"),
        P(("parts", "space"), None, None),
        P("parts"),
        P(),
        P(("parts", "space"), None),
    )
    return jax.shard_map(
        body, mesh=mesh, in_specs=placed, out_specs=P("parts", "space", None), check_vma=False
    )
```

```python
import functools

import jax
import jax.numpy as jnp
from jax import lax
from jax.experimental import pallas as pl
from jax.experimental.pallas import tpu as pltpu
from jax.sharding import PartitionSpec as P


VMEM = pl.BlockSpec(memory_space=pltpu.VMEM)
HBM = pl.BlockSpec(memory_space=pltpu.HBM)
STREAMS = 2
ORDERS = (((0, 1, 2), (1, 2, 0)), ((0, 1, 2), (1, 0, 2)))
PARAMS = pltpu.CompilerParams(vmem_limit_bytes=20 << 20)


def swap(block, bit, odd_bit=None):
    count = lax.axis_size("space")
    bits = (bit, bit if odd_bit is None else odd_bit)
    return lax.ppermute(block, "space", [(i, i ^ bits[i & 1]) for i in range(count)])


def slip_kernel(coefficients_hbm, modes_hbm, slip_ref, coefficients_ref, modes_ref, semaphores):
    parts = semaphores.shape[0] - 1
    depth = modes_ref.shape[0] // parts
    first = pltpu.make_async_copy(coefficients_hbm, coefficients_ref, semaphores.at[parts])
    first.start()
    copies = []
    for part in range(parts):
        lines = pl.ds(part * depth, depth)
        copies.append(
            pltpu.make_async_copy(
                modes_hbm.at[lines], modes_ref.at[lines], semaphores.at[part]
            )
        )
        copies[part].start()
    first.wait()
    field = jnp.zeros(slip_ref.shape[1:], jnp.float32)
    for part in range(parts):
        lines = slice(part * depth, (part + 1) * depth)
        copies[part].wait()
        field += jnp.dot(
            coefficients_ref[:, lines], modes_ref[lines], preferred_element_type=jnp.float32
        )
    slip_ref[0] = jnp.exp(0.5 * field).astype(slip_ref.dtype)


def load(green_ref, part_ref, semaphore, start, parity):
    copy = pltpu.make_async_copy(
        green_ref.at[pl.ds(start, part_ref.shape[0]), :, parity], part_ref, semaphore
    )
    copy.start()
    return copy


def choose_kernel(columns, levels, index_hbm, green_ref, part_ref, chosen_ref, index_ref, semaphores):
    me = lax.axis_index("space")
    fetch = pltpu.make_async_copy(index_hbm, index_ref, semaphores.at[0])
    fetch.start()
    copy = load(green_ref, part_ref, semaphores.at[1], 0, 1 - (me & 1))
    group = index_ref.shape[1]
    fetch.wait()
    for side in range(2):
        row_ids = index_ref[pl.ds(me ^ side, 1), :]
        distance = (row_ids // columns) ^ me
        slot = (distance >> 1) | ((distance & 1) << (levels - 1))
        position = slot * columns + row_ids % columns
        for first in range(0, chosen_ref.shape[0], group):
            row = lax.broadcasted_iota(jnp.int32, (group, group), 0) + first
            chosen_ref[first : first + group, side * group : (side + 1) * group] = jnp.where(
                row == position, 1.0, 0.0
            ).astype(jnp.bfloat16)
    copy.wait()


def repeat_kernel(rows, green_ref, away_ref, own_ref, repeat_ref, semaphores):
    odd = lax.axis_index("space") & 1
    first = green_ref.shape[0] - away_ref.shape[0]
    copies = (
        load(green_ref, away_ref, semaphores.at[0], first, 1 - odd),
        load(green_ref, own_ref, semaphores.at[1], 0, odd),
    )
    source = lax.broadcasted_iota(jnp.int32, repeat_ref.shape, 0)
    target = lax.broadcasted_iota(jnp.int32, repeat_ref.shape, 1)
    near = (target >= source * rows) & (target < (source + 1) * rows)
    repeat_ref[...] = jnp.where(near, 1.0, 0.0).astype(jnp.bfloat16)
    for copy in copies:
        copy.wait()


def rest_kernel(green_ref, own_ref, semaphore):
    first = green_ref.shape[0] - own_ref.shape[0]
    load(green_ref, own_ref, semaphore, first, lax.axis_index("space") & 1).wait()


def widen(chosen_ref, repeat_ref, slip_ref, wide_ref):
    group, depth = repeat_ref.shape
    slip = jnp.concatenate([slip_ref[owner] for owner in range(slip_ref.shape[0])], axis=1)
    picked = jnp.dot(slip, chosen_ref[...], preferred_element_type=jnp.float32)
    picked = picked.astype(jnp.bfloat16)
    for side in range(2):
        wide_ref[:, side * depth : (side + 1) * depth] = jnp.dot(
            picked[:, side * group : (side + 1) * group],
            repeat_ref[...],
            preferred_element_type=jnp.float32,
        )


def fill_spread(rows, start, wide_ref, spread_ref):
    realizations, depth = wide_ref.shape
    wide = wide_ref[...]
    row_of = lax.broadcasted_iota(jnp.int32, (realizations, depth), 1) % rows
    for row in range(spread_ref.shape[0] // realizations):
        spread_ref[row * realizations : (row + 1) * realizations, :] = jnp.where(
            row_of == start + row, wide, 0.0
        ).astype(jnp.bfloat16)


def first_kernel(places, rows, chosen_ref, repeat_ref, slip_ref, *refs):
    parts, (out_ref, spread_ref, wide_ref) = refs[:-3], refs[-3:]
    widen(chosen_ref, repeat_ref, slip_ref, wide_ref)
    fill_spread(rows, 0, wide_ref, spread_ref)
    uplift_kernel(places, 0, spread_ref, *parts, out_ref)


def next_kernel(places, stream, rows, start, wide_ref, *refs):
    fill_spread(rows, start, wide_ref, refs[-1])
    uplift_kernel(places, stream, refs[-1], *refs[:-1])


def stage_bits(stream, odd, count):
    leading = ORDERS[stream][odd]
    return leading + tuple(range(len(leading), count))


def spread_bits(place, bits):
    return sum(((place >> stage) & 1) << bit for stage, bit in enumerate(bits))


def uplift_kernel(places, stream, spread_ref, *refs):
    parts, out_ref = refs[:-1], refs[-1]
    rows, width = parts[0].shape[2:]
    me = lax.axis_index("space")
    levels = parts[0].shape[1].bit_length() - 1
    even, odd = (stage_bits(stream, side, levels) for side in range(2))

    def block(place):
        pair = (me >> 1) ^ jnp.where(
            (me & 1) == 0, spread_bits(place, even), spread_bits(place, odd)
        )
        pieces = [ref[:, pair].reshape(ref.shape[0] * rows, width) for ref in parts]
        return jnp.concatenate(pieces, axis=0)

    columns = jnp.concatenate([block(place) for place in places], axis=1)
    value = jnp.dot(spread_ref[...], columns, preferred_element_type=jnp.float32)
    for slot in range(len(places)):
        part = value[:, slot * width : (slot + 1) * width].reshape(out_ref.shape[1:])
        out_ref[slot] = part.astype(out_ref.dtype)


def uplift_blocks(places, stream, realizations, dtype, spread, parts):
    width = parts[0].shape[3]
    lines = spread.shape[0] // realizations
    return pl.pallas_call(
        functools.partial(uplift_kernel, places, stream),
        out_shape=jax.ShapeDtypeStruct((len(places), lines, realizations, width), dtype),
        in_specs=[VMEM] * (1 + len(parts)),
        out_specs=VMEM,
        compiler_params=PARAMS,
    )(spread, *parts)


def bands_kernel(kernel_ref, bands_ref):
    taps = kernel_ref.shape[0]
    half = taps // 2
    width = bands_ref.shape[1] // 2
    weights = (kernel_ref[...] / jnp.sum(kernel_ref[...])).astype(jnp.bfloat16)
    first = lax.broadcasted_iota(jnp.int32, (taps, width), 0)
    second = lax.broadcasted_iota(jnp.int32, (taps, width), 1)
    mirror = jnp.where(first + second == taps - 1, 1.0, 0.0).astype(jnp.bfloat16)
    lines = jnp.dot(weights, mirror, preferred_element_type=jnp.float32)
    source = lax.broadcasted_iota(jnp.int32, (width, width), 0)
    target = lax.broadcasted_iota(jnp.int32, (width, width), 1)
    inside = jnp.abs(source - target) <= half
    for tap in range(-1, taps + 1):
        if 0 <= tap < taps:
            line = jnp.broadcast_to(lines[tap : tap + 1, :], (width, width))
            rolled = pltpu.roll(line, width - half, 1, stride=1, stride_axis=0)
            band = jnp.where(inside, rolled, 0.0).astype(jnp.bfloat16)
        else:
            band = jnp.zeros((width, width), jnp.bfloat16)
        if tap >= 0:
            bands_ref[tap * width : (tap + 1) * width, :width] = band
        if tap < taps:
            bands_ref[(tap + 1) * width : (tap + 2) * width, width:] = band


def smooth_kernel(half, bands_ref, mask_ref, beside_ref, across_ref, own_ref, out_ref, pairs_ref):
    rows, realizations, width = own_ref.shape
    odd = lax.axis_index("space") & 1

    def place(ref, first, start, count):
        for row in range(count):
            pair, side = divmod(start + row, 2)
            pairs_ref[
                pair * realizations : (pair + 1) * realizations,
                side * width : (side + 1) * width,
            ] = ref[first + row]

    for parity, before_ref, after_ref in ((0, across_ref, beside_ref), (1, beside_ref, across_ref)):

        @pl.when(odd == parity)
        def _():
            place(before_ref, rows - half, 0, half)
            place(after_ref, 0, half + rows, half)

    place(own_ref, 0, half, rows)
    depth = rows // 2 * realizations
    lines = jnp.concatenate(
        [
            pairs_ref[shift * realizations : shift * realizations + depth, :]
            for shift in range(half + 1)
        ],
        axis=1,
    )
    value = jnp.dot(lines, bands_ref[...], preferred_element_type=jnp.float32)
    value = value.reshape(rows // 2, realizations, 2 * width)
    both = jnp.stack([value[:, :, :width], value[:, :, width:]], axis=1)
    both = both.reshape(rows, realizations, width)
    mask = mask_ref[...].astype(jnp.float32)
    out_ref[...] = jnp.transpose(both, (1, 0, 2)) * mask[None]


def body(coefficients, kl_modes, green, sub_index, kernel, wet_mask):
    realizations, _ = coefficients.shape
    columns = kl_modes.shape[1]
    group, _, width = green.shape
    rows = wet_mask.shape[0]
    taps = kernel.shape[0]
    half = taps // 2
    count = lax.axis_size("space")
    levels = count.bit_length() - 1
    assert 1 << levels == count and half <= rows and levels >= 4
    green = green.reshape(group, count // 2, 2, rows, width)
    green = pltpu.with_memory_space_constraint(green, pltpu.HBM)

    slip = pl.pallas_call(
        slip_kernel,
        out_shape=jax.ShapeDtypeStruct((1, realizations, columns), jnp.bfloat16),
        in_specs=[HBM, HBM],
        out_specs=VMEM,
        scratch_shapes=[
            pltpu.VMEM(coefficients.shape, coefficients.dtype),
            pltpu.VMEM(kl_modes.shape, kl_modes.dtype),
            pltpu.SemaphoreType.DMA((3,)),
        ],
        compiler_params=PARAMS,
    )(
        pltpu.with_memory_space_constraint(coefficients, pltpu.HBM),
        pltpu.with_memory_space_constraint(kl_modes, pltpu.HBM),
    )
    for level in (*range(1, levels), 0):
        arrived = swap(slip, 1 << level)
        slip = jnp.concatenate([slip, arrived], axis=0)

    def part(depth):
        return jax.ShapeDtypeStruct((depth, count // 2, rows, width), green.dtype)

    index = pltpu.with_memory_space_constraint(sub_index.reshape(-1, group), pltpu.HBM)
    away_low, chosen = pl.pallas_call(
        functools.partial(choose_kernel, columns, levels),
        out_shape=(
            part(group // 2),
            jax.ShapeDtypeStruct((sub_index.shape[0], 2 * group), jnp.bfloat16),
        ),
        in_specs=[HBM, HBM],
        out_specs=(VMEM, VMEM),
        scratch_shapes=[
            pltpu.VMEM(index.shape, index.dtype),
            pltpu.SemaphoreType.DMA((2,)),
        ],
        compiler_params=PARAMS,
    )(index, green)
    beside_low = swap(away_low, 1)
    away_high, own_low, repeat = pl.pallas_call(
        functools.partial(repeat_kernel, rows),
        out_shape=(
            part(group - group // 2),
            part(group // 4),
            jax.ShapeDtypeStruct((group, group * rows), jnp.bfloat16),
        ),
        in_specs=[HBM],
        out_specs=(VMEM, VMEM, VMEM),
        scratch_shapes=[pltpu.SemaphoreType.DMA((2,))],
        compiler_params=PARAMS,
    )(green)
    beside_high = swap(away_high, 1)
    own_high = pl.pallas_call(
        rest_kernel,
        out_shape=part(group - group // 4),
        in_specs=[HBM],
        out_specs=VMEM,
        scratch_shapes=[pltpu.SemaphoreType.DMA],
        compiler_params=PARAMS,
    )(green)
    parts = (own_low, own_high, beside_low, beside_high)
    bands = pl.pallas_call(
        bands_kernel,
        out_shape=jax.ShapeDtypeStruct(((taps + 1) * width, 2 * width), jnp.bfloat16),
        in_specs=[VMEM],
        out_specs=VMEM,
        compiler_params=PARAMS,
    )(kernel)

    cuts = [0, rows * 7 // 16, rows]
    wide = []

    def away_blocks(stream):
        sides = 2 * group * rows
        lines = cuts[stream + 1] - cuts[stream]
        shapes = (
            jax.ShapeDtypeStruct((count // 4, lines, realizations, width), jnp.bfloat16),
            jax.ShapeDtypeStruct((lines * realizations, sides), jnp.bfloat16),
        )
        if stream == 0:
            sent, spread, table = pl.pallas_call(
                functools.partial(first_kernel, places[1::2], rows),
                out_shape=(*shapes, jax.ShapeDtypeStruct((realizations, sides), jnp.float32)),
                in_specs=[VMEM] * (3 + len(parts)),
                out_specs=(VMEM, VMEM, VMEM),
                compiler_params=PARAMS,
            )(chosen, repeat, slip, *parts)
            wide.append(table)
            return sent, spread
        return pl.pallas_call(
            functools.partial(next_kernel, places[1::2], stream, rows, cuts[stream]),
            out_shape=shapes,
            in_specs=[VMEM] * (1 + len(parts)),
            out_specs=(VMEM, VMEM),
            compiler_params=PARAMS,
        )(wide[0], *parts)

    places = list(range(count // 2))
    streams = range(STREAMS)

    def stage_swap(block, stream, stage):
        even, odd = (stage_bits(stream, side, levels - 1)[stage] for side in range(2))
        return swap(block, 2 << even, 2 << odd)

    spreads, arrived, kept = [], [], []
    for stream in streams:
        sent, spread = away_blocks(stream)
        spreads.append(spread)
        arrived.append(stage_swap(sent, stream, 0))
    for stream in streams:
        block = uplift_blocks(
            places[::2], stream, realizations, jnp.float32, spreads[stream], parts
        )
        kept.append(block + arrived[stream].astype(jnp.float32))
    for level in range(2, levels):
        for stream in streams:
            pairs = kept[stream].reshape((-1, 2) + kept[stream].shape[1:])
            sent = pairs[:, 1].astype(jnp.bfloat16)
            moved = stage_swap(sent, stream, level - 1)
            kept[stream] = pairs[:, 0] + moved.astype(jnp.float32)
    seafloor = [block[0].astype(jnp.bfloat16) for block in kept]

    crossing = [(i, i + 1) for i in range(1, count - 1, 2)]
    crossing += [(target, source) for source, target in crossing]
    seafloor = jnp.concatenate(seafloor, axis=0)
    across = lax.ppermute(seafloor, "space", crossing)
    beside = swap(seafloor, 1)
    return pl.pallas_call(
        functools.partial(smooth_kernel, half),
        out_shape=jax.ShapeDtypeStruct((realizations, rows, width), jnp.float32),
        in_specs=[VMEM] * 5,
        out_specs=VMEM,
        scratch_shapes=[
            pltpu.VMEM(((rows // 2 + half) * realizations, 2 * width), jnp.bfloat16),
        ],
        compiler_params=PARAMS,
    )(bands, wet_mask, beside, across, seafloor)


def solution(mesh):
    placed = (
        P("parts", None),
        P("parts", "space"),
        P(("parts", "space"), None, None),
        P("parts"),
        P(),
        P(("parts", "space"), None),
    )
    return jax.shard_map(
        body, mesh=mesh, in_specs=placed, out_specs=P("parts", "space", None), check_vma=False
    )
```

```python
import functools

import jax
import jax.numpy as jnp
from jax import lax
from jax.experimental import pallas as pl
from jax.experimental.pallas import tpu as pltpu
from jax.sharding import PartitionSpec as P


VMEM = pl.BlockSpec(memory_space=pltpu.VMEM)
HBM = pl.BlockSpec(memory_space=pltpu.HBM)
STREAMS = 2
ORDERS = (((0, 1, 2), (1, 2, 0)), ((0, 1, 2), (1, 0, 2)))
PARAMS = pltpu.CompilerParams(vmem_limit_bytes=20 << 20)


def swap(block, bit, odd_bit=None):
    count = lax.axis_size("space")
    bits = (bit, bit if odd_bit is None else odd_bit)
    return lax.ppermute(block, "space", [(i, i ^ bits[i & 1]) for i in range(count)])


def slip_kernel(coefficients_hbm, modes_hbm, slip_ref, coefficients_ref, modes_ref, semaphores):
    parts = semaphores.shape[0] - 1
    depth = modes_ref.shape[0] // parts
    first = pltpu.make_async_copy(coefficients_hbm, coefficients_ref, semaphores.at[parts])
    first.start()
    copies = []
    for part in range(parts):
        lines = pl.ds(part * depth, depth)
        copies.append(
            pltpu.make_async_copy(
                modes_hbm.at[lines], modes_ref.at[lines], semaphores.at[part]
            )
        )
        copies[part].start()
    first.wait()
    field = jnp.zeros(slip_ref.shape[1:], jnp.float32)
    for part in range(parts):
        lines = slice(part * depth, (part + 1) * depth)
        copies[part].wait()
        field += jnp.dot(
            coefficients_ref[:, lines], modes_ref[lines], preferred_element_type=jnp.float32
        )
    slip_ref[0] = jnp.exp(0.5 * field).astype(slip_ref.dtype)


def load(green_ref, part_ref, semaphore, start, parity):
    copy = pltpu.make_async_copy(
        green_ref.at[pl.ds(start, part_ref.shape[0]), :, parity], part_ref, semaphore
    )
    copy.start()
    return copy


def choose_kernel(columns, levels, index_hbm, green_ref, part_ref, chosen_ref, index_ref, semaphores):
    me = lax.axis_index("space")
    fetch = pltpu.make_async_copy(index_hbm, index_ref, semaphores.at[0])
    fetch.start()
    copy = load(green_ref, part_ref, semaphores.at[1], 0, 1 - (me & 1))
    group = index_ref.shape[1]
    fetch.wait()
    for side in range(2):
        row_ids = index_ref[pl.ds(me ^ side, 1), :]
        distance = (row_ids // columns) ^ me
        slot = (distance >> 1) | ((distance & 1) << (levels - 1))
        position = slot * columns + row_ids % columns
        for first in range(0, chosen_ref.shape[0], group):
            row = lax.broadcasted_iota(jnp.int32, (group, group), 0) + first
            chosen_ref[first : first + group, side * group : (side + 1) * group] = jnp.where(
                row == position, 1.0, 0.0
            ).astype(jnp.bfloat16)
    copy.wait()


def repeat_kernel(rows, green_ref, away_ref, own_ref, repeat_ref, semaphores):
    odd = lax.axis_index("space") & 1
    first = green_ref.shape[0] - away_ref.shape[0]
    copies = (
        load(green_ref, away_ref, semaphores.at[0], first, 1 - odd),
        load(green_ref, own_ref, semaphores.at[1], 0, odd),
    )
    source = lax.broadcasted_iota(jnp.int32, repeat_ref.shape, 0)
    target = lax.broadcasted_iota(jnp.int32, repeat_ref.shape, 1)
    near = (target >= source * rows) & (target < (source + 1) * rows)
    repeat_ref[...] = jnp.where(near, 1.0, 0.0).astype(jnp.bfloat16)
    for copy in copies:
        copy.wait()


def rest_kernel(green_ref, own_ref, semaphore):
    first = green_ref.shape[0] - own_ref.shape[0]
    load(green_ref, own_ref, semaphore, first, lax.axis_index("space") & 1).wait()


def pick(slip_ref, chosen):
    slip = jnp.concatenate([slip_ref[owner] for owner in range(slip_ref.shape[0])], axis=1)
    return jnp.dot(slip, chosen, preferred_element_type=jnp.float32)


def early_kernel(chosen_ref, slip_ref, early_ref):
    early_ref[...] = pick(slip_ref, chosen_ref[: chosen_ref.shape[0] // 2, :])


def widen(chosen_ref, repeat_ref, slip_ref, early_ref, wide_ref):
    group, depth = repeat_ref.shape
    picked = early_ref[...] + pick(slip_ref, chosen_ref[chosen_ref.shape[0] // 2 :, :])
    picked = picked.astype(jnp.bfloat16)
    for side in range(2):
        wide_ref[:, side * depth : (side + 1) * depth] = jnp.dot(
            picked[:, side * group : (side + 1) * group],
            repeat_ref[...],
            preferred_element_type=jnp.float32,
        )


def fill_spread(rows, start, wide_ref, spread_ref):
    realizations, depth = wide_ref.shape
    wide = wide_ref[...]
    row_of = lax.broadcasted_iota(jnp.int32, (realizations, depth), 1) % rows
    for row in range(spread_ref.shape[0] // realizations):
        spread_ref[row * realizations : (row + 1) * realizations, :] = jnp.where(
            row_of == start + row, wide, 0.0
        ).astype(jnp.bfloat16)


def first_kernel(places, rows, chosen_ref, repeat_ref, slip_ref, early_ref, *refs):
    parts, (out_ref, spread_ref, wide_ref) = refs[:-3], refs[-3:]
    widen(chosen_ref, repeat_ref, slip_ref, early_ref, wide_ref)
    fill_spread(rows, 0, wide_ref, spread_ref)
    uplift_kernel(places, 0, spread_ref, *parts, out_ref)


def next_kernel(places, stream, rows, start, wide_ref, *refs):
    fill_spread(rows, start, wide_ref, refs[-1])
    uplift_kernel(places, stream, refs[-1], *refs[:-1])


def stage_bits(stream, odd, count):
    leading = ORDERS[stream][odd]
    return leading + tuple(range(len(leading), count))


def spread_bits(place, bits):
    return sum(((place >> stage) & 1) << bit for stage, bit in enumerate(bits))


def uplift_kernel(places, stream, spread_ref, *refs):
    parts, out_ref = refs[:-1], refs[-1]
    rows, width = parts[0].shape[2:]
    me = lax.axis_index("space")
    levels = parts[0].shape[1].bit_length() - 1
    even, odd = (stage_bits(stream, side, levels) for side in range(2))

    def block(place):
        pair = (me >> 1) ^ jnp.where(
            (me & 1) == 0, spread_bits(place, even), spread_bits(place, odd)
        )
        pieces = [ref[:, pair].reshape(ref.shape[0] * rows, width) for ref in parts]
        return jnp.concatenate(pieces, axis=0)

    columns = jnp.concatenate([block(place) for place in places], axis=1)
    value = jnp.dot(spread_ref[...], columns, preferred_element_type=jnp.float32)
    for slot in range(len(places)):
        part = value[:, slot * width : (slot + 1) * width].reshape(out_ref.shape[1:])
        out_ref[slot] = part.astype(out_ref.dtype)


def uplift_blocks(places, stream, realizations, dtype, spread, parts):
    width = parts[0].shape[3]
    lines = spread.shape[0] // realizations
    return pl.pallas_call(
        functools.partial(uplift_kernel, places, stream),
        out_shape=jax.ShapeDtypeStruct((len(places), lines, realizations, width), dtype),
        in_specs=[VMEM] * (1 + len(parts)),
        out_specs=VMEM,
        compiler_params=PARAMS,
    )(spread, *parts)


def bands_kernel(kernel_ref, bands_ref):
    taps = kernel_ref.shape[0]
    half = taps // 2
    width = bands_ref.shape[1] // 2
    weights = (kernel_ref[...] / jnp.sum(kernel_ref[...])).astype(jnp.bfloat16)
    first = lax.broadcasted_iota(jnp.int32, (taps, width), 0)
    second = lax.broadcasted_iota(jnp.int32, (taps, width), 1)
    mirror = jnp.where(first + second == taps - 1, 1.0, 0.0).astype(jnp.bfloat16)
    lines = jnp.dot(weights, mirror, preferred_element_type=jnp.float32)
    source = lax.broadcasted_iota(jnp.int32, (width, width), 0)
    target = lax.broadcasted_iota(jnp.int32, (width, width), 1)
    inside = jnp.abs(source - target) <= half
    for tap in range(-1, taps + 1):
        if 0 <= tap < taps:
            line = jnp.broadcast_to(lines[tap : tap + 1, :], (width, width))
            rolled = pltpu.roll(line, width - half, 1, stride=1, stride_axis=0)
            band = jnp.where(inside, rolled, 0.0).astype(jnp.bfloat16)
        else:
            band = jnp.zeros((width, width), jnp.bfloat16)
        if tap >= 0:
            bands_ref[tap * width : (tap + 1) * width, :width] = band
        if tap < taps:
            bands_ref[(tap + 1) * width : (tap + 2) * width, width:] = band


def smooth_kernel(half, bands_ref, mask_ref, beside_ref, across_ref, own_ref, out_ref, pairs_ref):
    rows, realizations, width = own_ref.shape
    odd = lax.axis_index("space") & 1

    def place(ref, first, start, count):
        for row in range(count):
            pair, side = divmod(start + row, 2)
            pairs_ref[
                pair * realizations : (pair + 1) * realizations,
                side * width : (side + 1) * width,
            ] = ref[first + row]

    for parity, before_ref, after_ref in ((0, across_ref, beside_ref), (1, beside_ref, across_ref)):

        @pl.when(odd == parity)
        def _():
            place(before_ref, rows - half, 0, half)
            place(after_ref, 0, half + rows, half)

    place(own_ref, 0, half, rows)
    depth = rows // 2 * realizations
    lines = jnp.concatenate(
        [
            pairs_ref[shift * realizations : shift * realizations + depth, :]
            for shift in range(half + 1)
        ],
        axis=1,
    )
    value = jnp.dot(lines, bands_ref[...], preferred_element_type=jnp.float32)
    value = value.reshape(rows // 2, realizations, 2 * width)
    both = jnp.stack([value[:, :, :width], value[:, :, width:]], axis=1)
    both = both.reshape(rows, realizations, width)
    mask = mask_ref[...].astype(jnp.float32)
    out_ref[...] = jnp.transpose(both, (1, 0, 2)) * mask[None]


def body(coefficients, kl_modes, green, sub_index, kernel, wet_mask):
    realizations, _ = coefficients.shape
    columns = kl_modes.shape[1]
    group, _, width = green.shape
    rows = wet_mask.shape[0]
    taps = kernel.shape[0]
    half = taps // 2
    count = lax.axis_size("space")
    levels = count.bit_length() - 1
    assert 1 << levels == count and half <= rows and levels >= 4
    green = green.reshape(group, count // 2, 2, rows, width)
    green = pltpu.with_memory_space_constraint(green, pltpu.HBM)

    slip = pl.pallas_call(
        slip_kernel,
        out_shape=jax.ShapeDtypeStruct((1, realizations, columns), jnp.bfloat16),
        in_specs=[HBM, HBM],
        out_specs=VMEM,
        scratch_shapes=[
            pltpu.VMEM(coefficients.shape, coefficients.dtype),
            pltpu.VMEM(kl_modes.shape, kl_modes.dtype),
            pltpu.SemaphoreType.DMA((3,)),
        ],
        compiler_params=PARAMS,
    )(
        pltpu.with_memory_space_constraint(coefficients, pltpu.HBM),
        pltpu.with_memory_space_constraint(kl_modes, pltpu.HBM),
    )
    for level in range(1, levels):
        arrived = swap(slip, 1 << level)
        slip = jnp.concatenate([slip, arrived], axis=0)
    last_slip = swap(slip, 1)

    def part(depth):
        return jax.ShapeDtypeStruct((depth, count // 2, rows, width), green.dtype)

    index = pltpu.with_memory_space_constraint(sub_index.reshape(-1, group), pltpu.HBM)
    away_low, chosen = pl.pallas_call(
        functools.partial(choose_kernel, columns, levels),
        out_shape=(
            part(group // 2),
            jax.ShapeDtypeStruct((sub_index.shape[0], 2 * group), jnp.bfloat16),
        ),
        in_specs=[HBM, HBM],
        out_specs=(VMEM, VMEM),
        scratch_shapes=[
            pltpu.VMEM(index.shape, index.dtype),
            pltpu.SemaphoreType.DMA((2,)),
        ],
        compiler_params=PARAMS,
    )(index, green)
    beside_low = swap(away_low, 1)
    away_high, own_low, repeat = pl.pallas_call(
        functools.partial(repeat_kernel, rows),
        out_shape=(
            part(group - group // 2),
            part(group // 4),
            jax.ShapeDtypeStruct((group, group * rows), jnp.bfloat16),
        ),
        in_specs=[HBM],
        out_specs=(VMEM, VMEM, VMEM),
        scratch_shapes=[pltpu.SemaphoreType.DMA((2,))],
        compiler_params=PARAMS,
    )(green)
    beside_high = swap(away_high, 1)
    own_high = pl.pallas_call(
        rest_kernel,
        out_shape=part(group - group // 4),
        in_specs=[HBM],
        out_specs=VMEM,
        scratch_shapes=[pltpu.SemaphoreType.DMA],
        compiler_params=PARAMS,
    )(green)
    parts = (own_low, own_high, beside_low, beside_high)
    bands = pl.pallas_call(
        bands_kernel,
        out_shape=jax.ShapeDtypeStruct(((taps + 1) * width, 2 * width), jnp.bfloat16),
        in_specs=[VMEM],
        out_specs=VMEM,
        compiler_params=PARAMS,
    )(kernel)

    cuts = [0, rows * 7 // 16, rows]
    early = pl.pallas_call(
        early_kernel,
        out_shape=jax.ShapeDtypeStruct((realizations, 2 * group), jnp.float32),
        in_specs=[VMEM] * 2,
        out_specs=VMEM,
        compiler_params=PARAMS,
    )(chosen, slip)
    wide = []

    def away_blocks(stream):
        sides = 2 * group * rows
        lines = cuts[stream + 1] - cuts[stream]
        shapes = (
            jax.ShapeDtypeStruct((count // 4, lines, realizations, width), jnp.bfloat16),
            jax.ShapeDtypeStruct((lines * realizations, sides), jnp.bfloat16),
        )
        if stream == 0:
            sent, spread, table = pl.pallas_call(
                functools.partial(first_kernel, places[1::2], rows),
                out_shape=(*shapes, jax.ShapeDtypeStruct((realizations, sides), jnp.float32)),
                in_specs=[VMEM] * (4 + len(parts)),
                out_specs=(VMEM, VMEM, VMEM),
                compiler_params=PARAMS,
            )(chosen, repeat, last_slip, early, *parts)
            wide.append(table)
            return sent, spread
        return pl.pallas_call(
            functools.partial(next_kernel, places[1::2], stream, rows, cuts[stream]),
            out_shape=shapes,
            in_specs=[VMEM] * (1 + len(parts)),
            out_specs=(VMEM, VMEM),
            compiler_params=PARAMS,
        )(wide[0], *parts)

    places = list(range(count // 2))
    streams = range(STREAMS)

    def stage_swap(block, stream, stage):
        even, odd = (stage_bits(stream, side, levels - 1)[stage] for side in range(2))
        return swap(block, 2 << even, 2 << odd)

    spreads, arrived, kept = [], [], []
    for stream in streams:
        sent, spread = away_blocks(stream)
        spreads.append(spread)
        arrived.append(stage_swap(sent, stream, 0))
    for stream in streams:
        block = uplift_blocks(
            places[::2], stream, realizations, jnp.float32, spreads[stream], parts
        )
        kept.append(block + arrived[stream].astype(jnp.float32))
    for level in range(2, levels):
        for stream in streams:
            pairs = kept[stream].reshape((-1, 2) + kept[stream].shape[1:])
            sent = pairs[:, 1].astype(jnp.bfloat16)
            moved = stage_swap(sent, stream, level - 1)
            kept[stream] = pairs[:, 0] + moved.astype(jnp.float32)
    seafloor = [block[0].astype(jnp.bfloat16) for block in kept]

    crossing = [(i, i + 1) for i in range(1, count - 1, 2)]
    crossing += [(target, source) for source, target in crossing]
    seafloor = jnp.concatenate(seafloor, axis=0)
    across = lax.ppermute(seafloor, "space", crossing)
    beside = swap(seafloor, 1)
    return pl.pallas_call(
        functools.partial(smooth_kernel, half),
        out_shape=jax.ShapeDtypeStruct((realizations, rows, width), jnp.float32),
        in_specs=[VMEM] * 5,
        out_specs=VMEM,
        scratch_shapes=[
            pltpu.VMEM(((rows // 2 + half) * realizations, 2 * width), jnp.bfloat16),
        ],
        compiler_params=PARAMS,
    )(bands, wet_mask, beside, across, seafloor)


def solution(mesh):
    placed = (
        P("parts", None),
        P("parts", "space"),
        P(("parts", "space"), None, None),
        P("parts"),
        P(),
        P(("parts", "space"), None),
    )
    return jax.shard_map(
        body, mesh=mesh, in_specs=placed, out_specs=P("parts", "space", None), check_vma=False
    )
```
